256 devices in a mesh: pts: 2 (over core), geo: 128 (over z, y, x).
Axes of the slice: x: 4, y: 4, z: 8, core: 2. Of those that a mesh axis runs over, the one named last changes fastest.
Arguments:
- points: bfloat16 [128, 1024, 256], P('geo', 'pts'), may hold values from -6 to 6
- result_grad: bfloat16 [128, 1024, 256], P('geo', 'pts'), may hold values from -6 to 6
- lists_one: int32 [128, 8, 4], P('geo', 'pts'), may hold values from 0 to 7, all different within a row
- lists_two: int32 [128, 8, 4], P('geo', 'pts'), may hold values from 0 to 7, all different within a row
- rotation: int32 [128, 1024], P('geo', 'pts'), may hold values from 0 to 1023, each once within a row
- gain_one: bfloat16 [256], replicated, may hold values from 0.25 to 1.75
- qkv_one: bfloat16 [256, 768], replicated, may hold values from -0.375 to 0.375
- out_one: bfloat16 [256, 256], replicated, may hold values from -0.375 to 0.375
- gain_two: bfloat16 [256], replicated, may hold values from 0.25 to 1.75
- qkv_two: bfloat16 [256, 768], replicated, may hold values from -0.375 to 0.375
- out_two: bfloat16 [256, 256], replicated, may hold values from -0.375 to 0.375
Outputs:
- result: bfloat16 [128, 1024, 256], P('geo', 'pts')
- points_grad: bfloat16 [128, 1024, 256], P('geo', 'pts')
- gain_one_grad: float32 [256], replicated
- qkv_one_grad: float32 [256, 768], replicated
- out_one_grad: float32 [256, 256], replicated
- gain_two_grad: float32 [256], replicated
- qkv_two_grad: float32 [256, 768], replicated
- out_two_grad: float32 [256, 256], replicated
The draws below stay inside these ranges and needn't reach their ends.
Inputs may be any that keep to these rules, and one draw needn't show every extreme that they name: `lists_one`: each ball lists 4 different balls of its geometry. `lists_two`: each ball lists 4 different balls of its geometry. `rotation`: each geometry's row is a permutation of its points.
All inputs are finite; a program needn't handle non-finite values.
Results may differ from the reference program's by a relative error of at most 0.012.
Values may be sent and summed in bfloat16 or wider, within the bound.
A program may use at most 64 MiB of HBM per device.

```python
import jax
import jax.numpy as jnp
from jax import lax

D = 256
HEADS = 4
BALL = 128
LISTED = 4
POINTS = 1024
BALLS = 8
GEOS = 128


def steps_of(own_key, shape, shards, smallest, top_value):
    level = 1.0
    for position, parts in shards:
        heights = jax.random.uniform(jax.random.fold_in(jax.random.fold_in(own_key, 6), position), (parts,), jnp.float32, smallest / len(shards), top_value / len(shards))
        level = level * jnp.repeat(jnp.exp(heights), shape[position] // parts).reshape((-1,) + (1,) * (len(shape) - 1 - position))
    return level


def choose_distinct(rng, rows, number_of, top, lift):
    order = jax.random.permutation(jax.random.fold_in(rng, 1), number_of)
    favour = order
    for power in range(3):
        favour = favour * favour // number_of
    favour = favour * lift // number_of
    chance = jax.random.randint(jax.random.fold_in(rng, 2), (rows, number_of), 0, 4096) + favour
    fixed_rows = jax.random.permutation(jax.random.fold_in(rng, 3), rows)[jnp.arange(number_of) % rows]
    chance = jnp.where(jnp.arange(rows)[:, None] == fixed_rows[None, :], 1 << 14, chance)
    score = chance * number_of + jnp.arange(number_of)
    return lax.top_k(score.astype(jnp.int32), top)[1].astype(jnp.int32)


def scatter_about(rng, dims, deviation, most, split=(), dtype=jnp.bfloat16):
    array = deviation * jax.random.normal(rng, dims, jnp.float32)
    if split:
        array = array * steps_of(rng, dims, split, -0.22, 0.18)
    return jnp.clip(array, -most, most).astype(dtype)


def setup_inputs(seed: int = 0) -> dict:
    arg_keys = jax.random.split(jax.random.key(seed), 12)
    return {
        "points": scatter_about(arg_keys[0], (GEOS, POINTS, D), 1.0, 6.0, ((0, 128), (1, 2))),
        "result_grad": scatter_about(arg_keys[1], (GEOS, POINTS, D), 1.0, 6.0, ((0, 128), (1, 2))),
        "lists_one": choose_distinct(arg_keys[2], GEOS * BALLS, BALLS, LISTED, 0).reshape((GEOS, BALLS, LISTED)),
        "lists_two": choose_distinct(arg_keys[3], GEOS * BALLS, BALLS, LISTED, 0).reshape((GEOS, BALLS, LISTED)),
        "rotation": jax.vmap(lambda own: jax.random.permutation(own, POINTS))(jax.random.split(arg_keys[4], GEOS)).reshape((GEOS, POINTS)).astype(jnp.int32),
        "gain_one": jnp.clip(1.0 + 0.15 * jax.random.normal(arg_keys[5], (D,), jnp.float32), 0.25, 1.75).astype(jnp.bfloat16),
        "qkv_one": scatter_about(arg_keys[6], (D, 3 * D), D ** -0.5, 0.375),
        "out_one": scatter_about(arg_keys[7], (D, D), D ** -0.5, 0.375),
        "gain_two": jnp.clip(1.0 + 0.15 * jax.random.normal(arg_keys[8], (D,), jnp.float32), 0.25, 1.75).astype(jnp.bfloat16),
        "qkv_two": scatter_about(arg_keys[9], (D, 3 * D), D ** -0.5, 0.375),
        "out_two": scatter_about(arg_keys[10], (D, D), D ** -0.5, 0.375),
    }


HIGH = lax.Precision.HIGHEST

def pick_rows(source, indices):
    return jnp.take(source, indices, axis=0)

def keep_cotangent(values):
    rounded = values.astype(jnp.bfloat16).astype(jnp.float32)
    return lax.stop_gradient(rounded) + (values - lax.stop_gradient(values))

def round_cotangent(values):
    rounded = values.astype(jnp.bfloat16).astype(jnp.float32)
    return lax.stop_gradient(values) + (rounded - lax.stop_gradient(rounded))

def prepare(inputs, gain, weight):
    meansq = lax.optimization_barrier(jnp.mean(inputs * inputs, axis=-1, keepdims=True))
    normed = (inputs * lax.rsqrt(meansq + 1e-06) * gain).astype(jnp.bfloat16).astype(jnp.float32)
    projected = jnp.einsum('gnd,de->gne', normed, weight, precision=HIGH)
    width = inputs.shape[-1]
    return (projected[..., :width].astype(jnp.bfloat16), keep_cotangent(projected[..., width:]))

def attend(inputs, queries, keyvals, listed, weight):
    groups, rows, width = inputs.shape
    local_balls = rows // BALL
    head_dim = width // HEADS
    query_blocks = queries.astype(jnp.float32).reshape(groups, local_balls, BALL, HEADS, head_dim)
    blocks = keyvals.reshape(groups, -1, BALL, 2, HEADS, head_dim)
    chosen = jax.vmap(pick_rows)(blocks, listed)
    chosen = chosen.reshape(groups, local_balls, LISTED * BALL, 2, HEADS, head_dim)
    products = jnp.einsum('gbqhd,gbkhd->gbhqk', query_blocks, chosen[:, :, :, 0], precision=HIGH)
    scores = round_cotangent(products) * head_dim ** (-0.5)
    topmost = lax.stop_gradient(lax.optimization_barrier(jnp.max(scores, axis=-1, keepdims=True)))
    exponent = jnp.exp(scores - topmost)
    probs = exponent / lax.optimization_barrier(jnp.sum(exponent, axis=-1, keepdims=True))
    probs = probs.astype(jnp.bfloat16).astype(jnp.float32)
    mixed = jnp.einsum('gbhqk,gbkhd->gbqhd', probs, chosen[:, :, :, 1], precision=HIGH)
    mixed = mixed.astype(jnp.bfloat16).astype(jnp.float32).reshape(groups, rows, width)
    output = jnp.einsum('gnd,de->gne', mixed, weight, precision=HIGH)
    return (inputs + output).astype(jnp.bfloat16)

def layer(rows, listed, gain, weight_in, weight_out):
    inputs = rows.astype(jnp.float32)
    queries, keyvals = prepare(inputs, gain, weight_in)
    return attend(inputs, queries, keyvals, listed, weight_out)

def reference(points, result_grad, lists_one, lists_two, rotation, gain_one, qkv_one, out_one, gain_two, qkv_two, out_two):
    weights = tuple((item.astype(jnp.float32) for item in (gain_one, qkv_one, out_one, gain_two, qkv_two, out_two)))

    def model(inputs, params):

        def one_geometry(packed):
            rows, first, second, order = packed
            hidden = layer(rows[None], first[None], params[0], params[1], params[2])
            moved = jnp.take(hidden[0], order, axis=0)[None]
            return layer(moved, second[None], params[3], params[4], params[5])[0]
        return lax.map(jax.checkpoint(one_geometry), (inputs, lists_one, lists_two, rotation))
    result, backward = jax.vjp(model, points, weights)
    points_grad, grads = backward(result_grad)
    return (result, points_grad, grads[0], grads[1], grads[2], grads[3], grads[4], grads[5])
```

```python
import functools

import jax
import jax.numpy as jnp
from jax import lax
from jax.experimental import pallas as pl
from jax.experimental.pallas import tpu as pltpu
from jax.sharding import PartitionSpec as P

HEADS = 4
BALL = 128
LISTED = 4
BALLS = 8
ROWS = BALL * BALLS
HALF = ROWS // 2
D = 256
OWN = 128
EPSILON = 1e-06
XY = 16
WIDE = 1152
CHUNK = 256 // XY
MESH = pl.DeviceIdType.MESH
F32 = jnp.float32
BF16 = jnp.bfloat16


def dot(a, b):
    return jnp.dot(a, b, preferred_element_type=F32)


def dot_nt(a, b):
    return lax.dot_general(a, b, (((1,), (1,)), ((), ())), preferred_element_type=F32)


def rows_of(b, size=BALL):
    return pl.ds(pl.multiple_of(b * size, size), size)


def layers_kernel(
    points,
    result_grad,
    lists_one,
    lists_two,
    rotation,
    gain_one,
    qkv_one,
    out_one,
    gain_two,
    qkv_two,
    out_two,
    result,
    points_grad,
    packed,
    x_all,
    g_all,
    lists_v,
    lists_s,
    rot_v,
    w_own,
    normed_t,
    q_st,
    kv_all,
    k_t,
    v_t,
    att,
    mix_t,
    mixed,
    dqkv,
    parts,
    ngrad,
    perm,
    perm_t,
    in_send,
    in_recv,
    own_sem,
    smem_sem,
    mix_send,
    mix_recv,
    ng_send,
    ng_recv,
):
    c = lax.axis_index("pts")
    other = 1 - c
    gains = (gain_one, gain_two)
    qkvs = (qkv_one, qkv_two)
    outs = (out_one, out_two)

    def remote(src, dst, send, recv):
        return pltpu.make_async_remote_copy(
            src_ref=src,
            dst_ref=dst,
            send_sem=send,
            recv_sem=recv,
            device_id={"pts": other},
            device_id_type=MESH,
        )

    barrier = pltpu.get_barrier_semaphore()
    pl.semaphore_signal(barrier, inc=1, device_id={"pts": other}, device_id_type=MESH)
    pl.semaphore_wait(barrier, 1)

    inputs = (
        (points.at[0], x_all.at[0, rows_of(c, HALF)]),
        (lists_one.at[0], lists_v.at[0, c]),
        (lists_two.at[0], lists_v.at[1, c]),
        (rotation, rot_v.at[c]),
        (result_grad.at[0], g_all.at[1, rows_of(c, HALF)]),
    )
    sent = [
        remote(src, dst, in_send.at[n], in_recv.at[n]) for n, (src, dst) in enumerate(inputs)
    ]
    kept = [
        pltpu.make_async_copy(src, dst, own_sem.at[n]) for n, (src, dst) in enumerate(inputs)
    ]
    for copy in sent:
        copy.start()
    for copy in kept:
        copy.start()

    col = pl.ds(pl.multiple_of(c * OWN, OWN), OWN)
    for i in range(2):
        for n in range(3):
            part = pl.ds(pl.multiple_of(n * D + c * OWN, OWN), OWN)
            w_own[i, :, n * OWN : (n + 1) * OWN] = qkvs[i][:, part]
    parts[LISTED * BALLS] = jnp.zeros((BALL, D), F32)

    lane = lax.broadcasted_iota(jnp.int32, (BALL, OWN), 1)
    first = lane < OWN // 2

    def stacked(value):
        zero = jnp.zeros_like(value)
        return jnp.concatenate(
            [jnp.where(first, value, zero), jnp.where(first, zero, value)], axis=0
        )

    def unstacked_t(value):
        return jnp.concatenate([value[: OWN // 2, :BALL], value[OWN // 2 :, BALL:]], axis=0)

    def project(i, b):
        x = x_all[i, rows_of(b)].astype(F32)
        gain = gains[i][...].astype(F32)
        factor = lax.rsqrt(jnp.mean(x * x, axis=-1, keepdims=True) + EPSILON)
        normed = x * factor * gain
        normed_t[i, :, rows_of(b)] = normed.T.astype(BF16)
        qkv = dot(normed.astype(BF16), w_own[i])
        q = qkv[:, :OWN].astype(BF16).astype(F32) * 0.125
        q_st[i, b] = stacked(q).astype(BF16)
        kv_all[i, b] = qkv[:, OWN:].astype(BF16)
        k_t[i, b] = qkv[:, OWN : 2 * OWN].T.astype(BF16)
        v_t[i, b] = qkv[:, 2 * OWN :].T.astype(BF16)

    def listed(i, b):
        return [lists_s[i, b // 4, b % 4, n] for n in range(LISTED)]

    def attend(i, b):
        ids = listed(i, b)
        keys = jnp.concatenate([kv_all[i, t, :, :OWN] for t in ids], axis=0)
        scores = dot_nt(keys, q_st[i, b])
        top = jnp.max(scores, axis=0, keepdims=True)
        exponent = jnp.exp(scores - top)
        attention = exponent * (1.0 / jnp.sum(exponent, axis=0, keepdims=True))
        att[i, b] = attention
        values_t = jnp.concatenate([v_t[i, t] for t in ids], axis=1)
        own_t = unstacked_t(dot(values_t, attention.astype(BF16)))
        mix_t[i, :, rows_of(b)] = own_t.astype(BF16)
        mixed[i, c, rows_of(b)] = own_t.T.astype(BF16)

    def mix_copy(i, b, slot):
        ref = mixed.at[i, c, rows_of(b)]
        return remote(ref, ref, mix_send.at[i, slot], mix_recv.at[i, slot])

    def project_out(i, b):
        both = jnp.concatenate([mixed[i, 0, rows_of(b)], mixed[i, 1, rows_of(b)]], axis=1)
        x = x_all[i, rows_of(b)].astype(F32)
        return (x + dot(both, outs[i][...])).astype(BF16)

    kept[0].wait()
    lax.fori_loop(0, 4, lambda j, _: project(0, c * 4 + j), None)
    for n in (1, 2, 3):
        kept[n].wait()
        sent[n].wait()
    to_smem = pltpu.make_async_copy(lists_v, lists_s, smem_sem)
    to_smem.start()
    sent[0].wait()
    lax.fori_loop(0, 4, lambda j, _: project(0, other * 4 + j), None)
    to_smem.wait()

    def attend_send(j, _):
        attend(0, j)
        mix_copy(0, j, j).start()

    lax.fori_loop(0, BALLS, attend_send, None)

    rot_row = jnp.concatenate([rot_v[0], rot_v[1]], axis=1)

    def build_t(b, _):
        ids = lax.broadcasted_iota(jnp.int32, (BALL, ROWS), 0) + b * BALL
        perm_t[rows_of(b)] = jnp.where(ids == rot_row, 1.0, 0.0).astype(BF16)

    lax.fori_loop(0, BALLS, build_t, None)
    for b in range(BALLS):
        here = rot_row[:, b * BALL : (b + 1) * BALL].astype(F32)
        column = jnp.broadcast_to(here, (BALL, BALL)).T
        for n in range(BALLS):
            ids = (lane + n * BALL).astype(F32)
            perm[b * BALL : (b + 1) * BALL, n * BALL : (n + 1) * BALL] = jnp.where(
                ids == column, 1.0, 0.0
            ).astype(BF16)

    def hidden_rows(b, _):
        mix_copy(0, b, b).wait()
        x_all[2, rows_of(b)] = project_out(0, b)

    lax.fori_loop(0, BALLS, hidden_rows, None)

    def rotate(b, _):
        x_all[1, rows_of(b)] = dot(perm[rows_of(b)], x_all[2]).astype(BF16)
        project(1, b)

    lax.fori_loop(0, BALLS, rotate, None)

    def attend_two(j, _):
        attend(1, other * 4 + j)
        mix_copy(1, other * 4 + j, j).start()

    lax.fori_loop(0, 4, attend_two, None)
    lax.fori_loop(0, 4, lambda j, _: attend(1, c * 4 + j), None)

    def result_rows(j, _):
        mix_copy(1, other * 4 + j, j).wait()
        result[0, rows_of(j)] = project_out(1, c * 4 + j)

    lax.fori_loop(0, 4, result_rows, None)
    kept[4].wait()
    sent[4].wait()

    def attend_back(i, b):
        ids = listed(i, b)
        mixed_grad = stacked(dot_nt(g_all[i, rows_of(b)], outs[i][col, :])).astype(BF16)
        values = jnp.concatenate([kv_all[i, t, :, OWN:] for t in ids], axis=0)
        weights_grad = dot_nt(values, mixed_grad)
        attention = att[i, b]
        inner = jnp.sum(attention * weights_grad, axis=0, keepdims=True)
        scores_grad = (attention * (weights_grad - inner)).astype(BF16)
        values_grad = dot(attention.astype(BF16), mixed_grad)
        keys_grad = dot(scores_grad, q_st[i, b])
        for n in range(LISTED):
            parts[b * LISTED + n, :, :OWN] = keys_grad[n * BALL : (n + 1) * BALL]
            parts[b * LISTED + n, :, OWN:] = values_grad[n * BALL : (n + 1) * BALL]
        keys_t = jnp.concatenate([k_t[i, t] for t in ids], axis=1)
        query_grad_t = unstacked_t(dot(keys_t, scores_grad)) * 0.125
        dqkv[rows_of(b), :OWN] = query_grad_t.T.astype(BF16)

    def gather_parts(i, t):
        total = jnp.zeros((BALL, D), F32)
        for b in range(BALLS):
            at = jnp.int32(LISTED * BALLS)
            for n in range(LISTED):
                at = jnp.where(lists_s[i, b // 4, b % 4, n] == t, b * LISTED + n, at)
            total = total + parts[at]
        dqkv[rows_of(t), OWN:] = total.astype(BF16)

    def ng_copy(i, b, slot):
        ref = ngrad.at[i, c, rows_of(b)]
        return remote(ref, ref, ng_send.at[i, slot], ng_recv.at[i, slot])

    def partial_rows(i, b):
        ngrad[i, c, rows_of(b)] = dot_nt(dqkv[rows_of(b)], w_own[i]).astype(BF16)

    def weight_grads(i):
        at = i * 512
        weight = dot(normed_t[i], dqkv[...]).astype(BF16)
        packed[:, at : at + 3 * OWN] = weight
        out_grad = dot(mix_t[i], g_all[i]).astype(BF16)
        packed[:OWN, at + 3 * OWN : at + 4 * OWN] = out_grad[:, :OWN]
        packed[OWN:, at + 3 * OWN : at + 4 * OWN] = out_grad[:, OWN:]

    def row_grads(i, b):
        x = x_all[i, rows_of(b)].astype(F32)
        gain = gains[i][...].astype(F32)
        factor = lax.rsqrt(jnp.mean(x * x, axis=-1, keepdims=True) + EPSILON)
        grad = ngrad[i, 0, rows_of(b)].astype(F32) + ngrad[i, 1, rows_of(b)].astype(F32)
        grad = grad.astype(BF16).astype(F32)
        scaled = grad * gain
        inner = jnp.mean(scaled * x, axis=-1, keepdims=True)
        inputs_grad = factor * scaled - x * (factor * factor * factor) * inner
        rows = (g_all[i, rows_of(b)].astype(F32) + inputs_grad).astype(BF16)
        return rows, jnp.sum(grad * (x * factor), axis=0, keepdims=True)

    lax.fori_loop(0, BALLS, lambda b, _: attend_back(1, b), None)
    lax.fori_loop(0, BALLS, lambda t, _: gather_parts(1, t), None)

    def partial_two(b, _):
        partial_rows(1, b)
        ng_copy(1, b, b).start()

    lax.fori_loop(0, BALLS, partial_two, None)
    weight_grads(1)

    def rows_two(b, total):
        ng_copy(1, b, b).wait()
        rows, gain_part = row_grads(1, b)
        x_all[2, rows_of(b)] = rows
        mine = ((b // 4) == c).astype(F32)
        return total + gain_part * mine

    gain_two_part = lax.fori_loop(0, BALLS, rows_two, jnp.zeros((1, D), F32))

    def unrotate(b, _):
        g_all[0, rows_of(b)] = dot(perm_t[rows_of(b)], x_all[2]).astype(BF16)

    lax.fori_loop(0, BALLS, unrotate, None)
    lax.fori_loop(0, BALLS, lambda b, _: attend_back(0, b), None)
    lax.fori_loop(0, BALLS, lambda t, _: gather_parts(0, t), None)

    def partial_one(j, _):
        partial_rows(0, other * 4 + j)
        ng_copy(0, other * 4 + j, j).start()

    lax.fori_loop(0, 4, partial_one, None)
    lax.fori_loop(0, 4, lambda j, _: partial_rows(0, c * 4 + j), None)
    weight_grads(0)

    def rows_one(j, total):
        ng_copy(0, other * 4 + j, j).wait()
        rows, gain_part = row_grads(0, c * 4 + j)
        points_grad[0, rows_of(j)] = rows
        return total + gain_part

    gain_one_part = lax.fori_loop(0, 4, rows_one, jnp.zeros((1, D), F32))
    one = jnp.broadcast_to(gain_one_part, (OWN, D)).T
    two = jnp.broadcast_to(gain_two_part, (OWN, D)).T
    wide = lax.broadcasted_iota(jnp.int32, (D, OWN), 1)
    packed[:, 1024:] = jnp.where(wide < OWN // 2, one, two).astype(BF16)


def sum_kernel(
    planes,
    packed,
    gain_one,
    qkv_one,
    out_one,
    gain_two,
    qkv_two,
    out_two,
    arrived,
    along_z,
    full,
    send_xy,
    recv_xy,
    send_z,
    recv_z,
    send_all,
    recv_all,
    send_core,
    recv_core,
):
    c = lax.axis_index("pts")
    geo = lax.axis_index("geo")
    z = geo // XY
    xy = geo % XY

    def near(k):
        return {"geo": z * XY + (xy + k) % XY}

    def deep(k):
        return {"geo": ((z + k) % planes) * XY + xy}

    def remote(src, dst, send, recv, device):
        return pltpu.make_async_remote_copy(
            src_ref=src,
            dst_ref=dst,
            send_sem=send,
            recv_sem=recv,
            device_id=device,
            device_id_type=MESH,
        )

    barrier = pltpu.get_barrier_semaphore()
    for k in range(1, XY):
        pl.semaphore_signal(barrier, inc=1, device_id=near(k), device_id_type=MESH)
    for k in range(1, planes):
        pl.semaphore_signal(barrier, inc=1, device_id=deep(k), device_id_type=MESH)
    pl.semaphore_signal(barrier, inc=1, device_id={"pts": 1 - c}, device_id_type=MESH)
    pl.semaphore_wait(barrier, XY + planes - 1)

    first = []
    for k in range(1, XY):
        peer = (xy + k) % XY
        first.append(
            remote(
                packed.at[rows_of(peer, CHUNK)],
                arrived.at[k - 1],
                send_xy.at[k - 1],
                recv_xy.at[k - 1],
                near(k),
            )
        )
        first[-1].start()
    total = packed[rows_of(xy, CHUNK)].astype(F32)
    for k in range(1, XY):
        first[k - 1].wait()
        total = total + arrived[k - 1].astype(F32)
    along_z[z] = total.astype(BF16)

    second = []
    for k in range(1, planes):
        second.append(
            remote(
                along_z.at[z], along_z.at[z], send_z.at[k - 1], recv_z.at[k - 1], deep(k)
            )
        )
        second[-1].start()
    for copy in second:
        copy.wait()
    total = along_z[0].astype(F32)
    for k in range(1, planes):
        total = total + along_z[k].astype(F32)
    full[c, rows_of(xy, CHUNK)] = total.astype(BF16)

    mine = full.at[c, rows_of(xy, CHUNK)]
    third = []
    for k in range(1, XY):
        third.append(remote(mine, mine, send_all.at[k - 1], recv_all.at[k - 1], near(k)))
        third[-1].start()
    across = []
    for k in range(XY):
        if k:
            third[k - 1].wait_recv()
        piece = full.at[c, rows_of((xy - k + XY) % XY, CHUNK)]
        across.append(
            remote(piece, piece, send_core.at[k], recv_core.at[k], {"pts": 1 - c})
        )
        across[-1].start()
    for copy in third:
        copy.wait_send()
    for copy in across:
        copy.wait()

    for at, qkv, out in ((0, qkv_one, out_one), (512, qkv_two, out_two)):
        for core in range(2):
            for n in range(3):
                qkv[:, n * D + core * OWN : n * D + (core + 1) * OWN] = full[
                    core, :, at + n * OWN : at + (n + 1) * OWN
                ].astype(F32)
            here = slice(core * OWN, (core + 1) * OWN)
            out[here, :OWN] = full[core, :OWN, at + 3 * OWN : at + 4 * OWN].astype(F32)
            out[here, OWN:] = full[core, OWN:, at + 3 * OWN : at + 4 * OWN].astype(F32)
    gains = (full[0, :, 1024:].astype(F32) + full[1, :, 1024:].astype(F32)).T
    gain_one[...] = gains[:1]
    gain_two[...] = gains[OWN // 2 : OWN // 2 + 1]


def vmem():
    return pl.BlockSpec(memory_space=pltpu.VMEM)


def layers_call(*args):
    return pl.pallas_call(
        layers_kernel,
        name="layers",
        out_shape=(
            jax.ShapeDtypeStruct((1, HALF, D), BF16),
            jax.ShapeDtypeStruct((1, HALF, D), BF16),
            jax.ShapeDtypeStruct((D, WIDE), BF16),
        ),
        in_specs=[vmem()] * 11,
        out_specs=(vmem(),) * 3,
        scratch_shapes=[
            pltpu.VMEM((3, ROWS, D), BF16),
            pltpu.VMEM((2, ROWS, D), BF16),
            pltpu.VMEM((2, 2, 4, LISTED), jnp.int32),
            pltpu.SMEM((2, 2, 4, LISTED), jnp.int32),
            pltpu.VMEM((2, 1, HALF), jnp.int32),
            pltpu.VMEM((2, D, 3 * OWN), BF16),
            pltpu.VMEM((2, D, ROWS), BF16),
            pltpu.VMEM((2, BALLS, 2 * BALL, OWN), BF16),
            pltpu.VMEM((2, BALLS, BALL, 2 * OWN), BF16),
            pltpu.VMEM((2, BALLS, OWN, BALL), BF16),
            pltpu.VMEM((2, BALLS, OWN, BALL), BF16),
            pltpu.VMEM((2, BALLS, LISTED * BALL, 2 * BALL), F32),
            pltpu.VMEM((2, OWN, ROWS), BF16),
            pltpu.VMEM((2, 2, ROWS, OWN), BF16),
            pltpu.VMEM((ROWS, 3 * OWN), BF16),
            pltpu.VMEM((LISTED * BALLS + 1, BALL, D), F32),
            pltpu.VMEM((2, 2, ROWS, D), BF16),
            pltpu.VMEM((ROWS, ROWS), BF16),
            pltpu.VMEM((ROWS, ROWS), BF16),
            pltpu.SemaphoreType.DMA((5,)),
            pltpu.SemaphoreType.DMA((5,)),
            pltpu.SemaphoreType.DMA((5,)),
            pltpu.SemaphoreType.DMA,
            pltpu.SemaphoreType.DMA((2, BALLS)),
            pltpu.SemaphoreType.DMA((2, BALLS)),
            pltpu.SemaphoreType.DMA((2, BALLS)),
            pltpu.SemaphoreType.DMA((2, BALLS)),
        ],
        compiler_params=pltpu.CompilerParams(
            collective_id=0, has_side_effects=True, vmem_limit_bytes=56 << 20
        ),
    )(*args)


def sums_call(packed, planes):
    shapes = (
        jax.ShapeDtypeStruct((1, D), F32),
        jax.ShapeDtypeStruct((D, 3 * D), F32),
        jax.ShapeDtypeStruct((D, D), F32),
    )
    return pl.pallas_call(
        functools.partial(sum_kernel, planes),
        name="sums",
        out_shape=shapes + shapes,
        in_specs=[vmem()],
        out_specs=(vmem(),) * 6,
        scratch_shapes=[
            pltpu.VMEM((XY - 1, CHUNK, WIDE), BF16),
            pltpu.VMEM((planes, CHUNK, WIDE), BF16),
            pltpu.VMEM((2, D, WIDE), BF16),
            pltpu.SemaphoreType.DMA((XY - 1,)),
            pltpu.SemaphoreType.DMA((XY - 1,)),
            pltpu.SemaphoreType.DMA((max(planes - 1, 1),)),
            pltpu.SemaphoreType.DMA((max(planes - 1, 1),)),
            pltpu.SemaphoreType.DMA((XY - 1,)),
            pltpu.SemaphoreType.DMA((XY - 1,)),
            pltpu.SemaphoreType.DMA((XY,)),
            pltpu.SemaphoreType.DMA((XY,)),
        ],
        compiler_params=pltpu.CompilerParams(
            collective_id=1, has_side_effects=True, vmem_limit_bytes=32 << 20
        ),
    )(packed)


def local(
    points,
    result_grad,
    lists_one,
    lists_two,
    rotation,
    gain_one,
    qkv_one,
    out_one,
    gain_two,
    qkv_two,
    out_two,
):
    result, points_grad, packed = layers_call(
        points,
        result_grad,
        lists_one,
        lists_two,
        rotation,
        gain_one.reshape(1, D),
        qkv_one,
        out_one,
        gain_two.reshape(1, D),
        qkv_two,
        out_two,
    )
    grads = sums_call(packed, lax.axis_size("geo") // XY)
    return (
        result,
        points_grad,
        grads[0].reshape(D),
        grads[1],
        grads[2],
        grads[3].reshape(D),
        grads[4],
        grads[5],
    )


def solution(mesh):
    rows = P("geo", "pts", None)
    placed = (rows, rows, rows, rows, P("geo", "pts"), P(), P(), P(), P(), P(), P())
    return jax.shard_map(
        local,
        mesh=mesh,
        in_specs=placed,
        out_specs=(rows, rows, P(), P(), P(), P(), P(), P()),
        check_vma=False,
    )
```

```python
import functools

import jax
import jax.numpy as jnp
from jax import lax
from jax.experimental import pallas as pl
from jax.experimental.pallas import tpu as pltpu
from jax.sharding import PartitionSpec as P

HEADS = 4
BALL = 128
LISTED = 4
BALLS = 8
ROWS = BALL * BALLS
HALF = ROWS // 2
D = 256
OWN = 128
EPSILON = 1e-06
XY = 16
MESH = pl.DeviceIdType.MESH
F32 = jnp.float32
BF16 = jnp.bfloat16


def dot(a, b):
    return jnp.dot(a, b, preferred_element_type=F32)


def dot_nt(a, b):
    return lax.dot_general(a, b, (((1,), (1,)), ((), ())), preferred_element_type=F32)


def rows_of(b, size=BALL):
    return pl.ds(pl.multiple_of(b * size, size), size)


def layers_kernel(
    near_count,
    planes,
    points,
    result_grad,
    lists_one,
    lists_two,
    rotation,
    gain_one,
    qkv_one,
    out_one,
    gain_two,
    qkv_two,
    out_two,
    result,
    points_grad,
    full_early,
    full_late,
    gain_sums,
    x_all,
    g_all,
    lists_v,
    lists_s,
    rot_v,
    w_own,
    w_out,
    normed_t,
    q_st,
    kv_all,
    k_t,
    v_t,
    att,
    mix_t,
    mixed,
    dqkv,
    parts,
    ngrad,
    perm,
    perm_t,
    early,
    late,
    near_early,
    near_late,
    deep_early,
    deep_late,
    near_gain,
    deep_gain,
    in_send,
    in_recv,
    own_sem,
    load_sem,
    smem_sem,
    mix_send,
    mix_recv,
    ng_send,
    ng_recv,
    send_xy,
    recv_xy,
    send_z,
    recv_z,
    send_all,
    recv_all,
    send_core,
    recv_core,
):
    c = lax.axis_index("pts")
    other = 1 - c
    geo = lax.axis_index("geo")
    z = geo // near_count
    xy = geo % near_count
    chunk = D // near_count
    gains = (gain_one, gain_two)
    qkvs = (qkv_one, qkv_two)
    outs = (out_one, out_two)

    def copy_to(device, src, dst, send, recv):
        return pltpu.make_async_remote_copy(
            src_ref=src,
            dst_ref=dst,
            send_sem=send,
            recv_sem=recv,
            device_id=device,
            device_id_type=MESH,
        )

    def remote(src, dst, send, recv):
        return copy_to({"pts": other}, src, dst, send, recv)

    def near(k):
        return {"geo": z * near_count + (xy + k) % near_count}

    def deep(k):
        return {"geo": ((z + k) % planes) * near_count + xy}

    barrier = pltpu.get_barrier_semaphore()
    pl.semaphore_signal(barrier, inc=1, device_id={"pts": other}, device_id_type=MESH)
    for k in range(1, near_count):
        pl.semaphore_signal(barrier, inc=1, device_id=near(k), device_id_type=MESH)
    for k in range(1, planes):
        pl.semaphore_signal(barrier, inc=1, device_id=deep(k), device_id_type=MESH)

    inputs = (
        (points.at[0], x_all.at[0, rows_of(c, HALF)]),
        (lists_one.at[0], lists_v.at[0, c]),
        (lists_two.at[0], lists_v.at[1, c]),
        (rotation, rot_v.at[c]),
        (result_grad.at[0], g_all.at[1, rows_of(c, HALF)]),
    )
    kept = [
        pltpu.make_async_copy(src, dst, own_sem.at[n]) for n, (src, dst) in enumerate(inputs)
    ]
    sent = [
        remote(src, dst, in_send.at[n], in_recv.at[n]) for n, (src, dst) in enumerate(inputs)
    ]
    loads = []
    for i in range(2):
        for n in range(3):
            part = pl.ds(pl.multiple_of(n * D + c * OWN, OWN), OWN)
            loads.append(
                pltpu.make_async_copy(
                    qkvs[i].at[:, part],
                    w_own.at[i, :, n * OWN : (n + 1) * OWN],
                    load_sem.at[4 * i + n],
                )
            )
        loads.append(pltpu.make_async_copy(outs[i], w_out.at[i], load_sem.at[4 * i + 3]))
    kept[0].start()
    for copy in loads[:3]:
        copy.start()
    for copy in kept[1:] + loads[3:]:
        copy.start()
    parts[LISTED * BALLS] = jnp.zeros((BALL, D), F32)
    col = pl.ds(pl.multiple_of(c * OWN, OWN), OWN)

    lane = lax.broadcasted_iota(jnp.int32, (BALL, OWN), 1)
    first = lane < OWN // 2

    def stacked(value):
        zero = jnp.zeros_like(value)
        return jnp.concatenate(
            [jnp.where(first, value, zero), jnp.where(first, zero, value)], axis=0
        )

    def unstacked_t(value):
        return jnp.concatenate([value[: OWN // 2, :BALL], value[OWN // 2 :, BALL:]], axis=0)

    def project(i, b):
        x = x_all[i, rows_of(b)].astype(F32)
        gain = gains[i][...].astype(F32).reshape(1, D)
        factor = lax.rsqrt(jnp.mean(x * x, axis=-1, keepdims=True) + EPSILON)
        normed = x * factor * gain
        normed_t[i, :, rows_of(b)] = normed.T.astype(BF16)
        qkv = dot(normed.astype(BF16), w_own[i])
        q = qkv[:, :OWN].astype(BF16).astype(F32) * 0.125
        q_st[i, b] = stacked(q).astype(BF16)
        kv_all[i, b] = qkv[:, OWN:].astype(BF16)
        k_t[i, b] = qkv[:, OWN : 2 * OWN].T.astype(BF16)
        v_t[i, b] = qkv[:, 2 * OWN :].T.astype(BF16)

    def listed(i, b):
        return [lists_s[i, b // 4, b % 4, n] for n in range(LISTED)]

    def attend(i, b):
        ids = listed(i, b)
        keys = jnp.concatenate([kv_all[i, t, :, :OWN] for t in ids], axis=0)
        scores = dot_nt(keys, q_st[i, b])
        top = jnp.max(scores, axis=0, keepdims=True)
        exponent = jnp.exp(scores - top)
        attention = exponent * (1.0 / jnp.sum(exponent, axis=0, keepdims=True))
        att[i, b] = attention
        values_t = jnp.concatenate([v_t[i, t] for t in ids], axis=1)
        own_t = unstacked_t(dot(values_t, attention.astype(BF16)))
        mix_t[i, :, rows_of(b)] = own_t.astype(BF16)
        mixed[i, c, rows_of(b)] = own_t.T.astype(BF16)

    def loop(count, body, unroll=4):
        lax.fori_loop(0, count, lambda j, _: body(j), None, unroll=unroll)

    def mix_copy(i, b, slot):
        ref = mixed.at[i, c, rows_of(b)]
        return remote(ref, ref, mix_send.at[i, slot], mix_recv.at[i, slot])

    def project_out(i, b):
        both = jnp.concatenate([mixed[i, 0, rows_of(b)], mixed[i, 1, rows_of(b)]], axis=1)
        x = x_all[i, rows_of(b)].astype(F32)
        return (x + dot(both, w_out[i])).astype(BF16)

    def build(b):
        here = rot_v[b // 4, :, rows_of(b % 4)].astype(F32)
        column = jnp.broadcast_to(here, (BALL, BALL)).T
        for n in range(BALLS):
            ids = (lane + n * BALL).astype(F32)
            perm[rows_of(b), n * BALL : (n + 1) * BALL] = jnp.where(
                ids == column, 1.0, 0.0
            ).astype(BF16)

    def build_t(b):
        ids = lax.broadcasted_iota(jnp.int32, (BALL, ROWS), 0) + b * BALL
        rot_row = jnp.concatenate([rot_v[0], rot_v[1]], axis=1)
        perm_t[rows_of(b)] = jnp.where(ids == rot_row, 1.0, 0.0).astype(BF16)

    kept[0].wait()
    for copy in loads[:3]:
        copy.wait()
    loop(4, lambda j: project(0, c * 4 + j))
    pl.semaphore_wait(barrier, near_count + planes - 1)
    for copy in sent:
        copy.start()
    for copy in kept[1:4]:
        copy.wait()
    loop(4, lambda j: build(c * 4 + j))
    for n in (1, 2, 3):
        sent[n].wait()
    to_smem = pltpu.make_async_copy(lists_v, lists_s, smem_sem)
    to_smem.start()
    sent[0].wait()
    loop(4, lambda j: project(0, other * 4 + j))
    to_smem.wait()
    for copy in loads[3:]:
        copy.wait()

    def attend_send(j):
        attend(0, j)
        mix_copy(0, j, j).start()

    loop(BALLS, attend_send)
    loop(BALLS, build_t)
    loop(4, lambda j: build(other * 4 + j))

    def hidden_rows(b):
        mix_copy(0, b, b).wait()
        x_all[2, rows_of(b)] = project_out(0, b)

    loop(BALLS, hidden_rows)
    x_all[1] = dot(perm[...], x_all[2]).astype(BF16)
    loop(BALLS, lambda b: project(1, b))

    def attend_two(j):
        attend(1, other * 4 + j)
        mix_copy(1, other * 4 + j, j).start()

    loop(4, attend_two)
    loop(4, lambda j: attend(1, c * 4 + j))

    def result_rows(j):
        mix_copy(1, other * 4 + j, j).wait()
        result[0, rows_of(j)] = project_out(1, c * 4 + j)

    loop(4, result_rows)
    kept[4].wait()
    sent[4].wait()

    def attend_back(i, b):
        ids = listed(i, b)
        mixed_grad = stacked(dot_nt(g_all[i, rows_of(b)], w_out[i, col, :])).astype(BF16)
        values = jnp.concatenate([kv_all[i, t, :, OWN:] for t in ids], axis=0)
        weights_grad = dot_nt(values, mixed_grad)
        attention = att[i, b]
        inner = jnp.sum(attention * weights_grad, axis=0, keepdims=True)
        scores_grad = (attention * (weights_grad - inner)).astype(BF16)
        values_grad = dot(attention.astype(BF16), mixed_grad)
        keys_grad = dot(scores_grad, q_st[i, b])
        for n in range(LISTED):
            parts[b * LISTED + n, :, :OWN] = keys_grad[n * BALL : (n + 1) * BALL]
            parts[b * LISTED + n, :, OWN:] = values_grad[n * BALL : (n + 1) * BALL]
        keys_t = jnp.concatenate([k_t[i, t] for t in ids], axis=1)
        query_grad_t = unstacked_t(dot(keys_t, scores_grad)) * 0.125
        dqkv[rows_of(b), :OWN] = query_grad_t.T.astype(BF16)

    def gather_parts(i, t):
        total = jnp.zeros((BALL, D), F32)
        for b in range(BALLS):
            at = jnp.int32(LISTED * BALLS)
            for n in range(LISTED):
                at = jnp.where(lists_s[i, b // 4, b % 4, n] == t, b * LISTED + n, at)
            total = total + parts[at]
        dqkv[rows_of(t), OWN:] = total.astype(BF16)

    def ng_copy(i, b, slot):
        ref = ngrad.at[i, c, rows_of(b)]
        return remote(ref, ref, ng_send.at[i, slot], ng_recv.at[i, slot])

    def partial_rows(i, b):
        ngrad[i, c, rows_of(b)] = dot_nt(dqkv[rows_of(b)], w_own[i]).astype(BF16)

    def row_grads(i, b):
        x = x_all[i, rows_of(b)].astype(F32)
        gain = gains[i][...].astype(F32).reshape(1, D)
        factor = lax.rsqrt(jnp.mean(x * x, axis=-1, keepdims=True) + EPSILON)
        grad = ngrad[i, 0, rows_of(b)].astype(F32) + ngrad[i, 1, rows_of(b)].astype(F32)
        grad = grad.astype(BF16).astype(F32)
        scaled = grad * gain
        inner = jnp.mean(scaled * x, axis=-1, keepdims=True)
        inputs_grad = factor * scaled - x * (factor * factor * factor) * inner
        rows = (g_all[i, rows_of(b)].astype(F32) + inputs_grad).astype(BF16)
        return rows, jnp.sum(grad * (x * factor), axis=0, keepdims=True)

    class Sum:
        def __init__(self, r, own, arrived, along, full):
            self.r, self.own, self.arrived, self.along, self.full = r, own, arrived, along, full
            at = rows_of(xy, chunk)
            self.first = [
                copy_to(
                    near(k),
                    own.at[rows_of((xy + k) % near_count, chunk)],
                    arrived.at[k - 1],
                    send_xy.at[r, k - 1],
                    recv_xy.at[r, k - 1],
                )
                for k in range(1, near_count)
            ]
            self.second = [
                copy_to(
                    deep(k), along.at[z], along.at[z], send_z.at[r, k - 1], recv_z.at[r, k - 1]
                )
                for k in range(1, planes)
            ]
            mine = full.at[c, at]
            self.third = [
                copy_to(near(k), mine, mine, send_all.at[r, k - 1], recv_all.at[r, k - 1])
                for k in range(1, near_count)
            ]
            pieces = [
                full.at[c, rows_of((xy - k + near_count) % near_count, chunk)]
                for k in range(near_count)
            ]
            self.across = [
                remote(piece, piece, send_core.at[r, k], recv_core.at[r, k])
                for k, piece in enumerate(pieces)
            ]

        def scatter(self):
            for copy in self.first:
                copy.start()

        def plane(self):
            total = self.own[rows_of(xy, chunk)].astype(F32)
            for k, copy in enumerate(self.first):
                copy.wait()
                total = total + self.arrived[k].astype(F32)
            self.along[z] = total.astype(BF16)
            for copy in self.second:
                copy.start()

        def column(self):
            for copy in self.second:
                copy.wait()
            total = self.along[0].astype(F32)
            for k in range(1, planes):
                total = total + self.along[k].astype(F32)
            self.full[c, rows_of(xy, chunk)] = total.astype(BF16)
            for copy in self.third:
                copy.start()
            self.across[0].start()

        def forward(self):
            for k, copy in enumerate(self.third):
                copy.wait_recv()
                self.across[k + 1].start()

        def finish(self):
            for copy in self.third:
                copy.wait_send()
            for copy in self.across:
                copy.wait()

    sum_early = Sum(0, early, near_early, deep_early, full_early)
    sum_late = Sum(1, late, near_late, deep_late, full_late)
    gain_first = [
        copy_to(
            near(k), near_gain.at[xy], near_gain.at[xy], send_xy.at[2, k - 1], recv_xy.at[2, k - 1]
        )
        for k in range(1, near_count)
    ]
    gain_second = [
        copy_to(deep(k), deep_gain.at[z], deep_gain.at[z], send_z.at[2, k - 1], recv_z.at[2, k - 1])
        for k in range(1, planes)
    ]
    gain_across = remote(
        gain_sums.at[c], gain_sums.at[c], send_core.at[2, 0], recv_core.at[2, 0]
    )

    loop(BALLS, lambda b: attend_back(1, b))
    loop(BALLS, lambda t: gather_parts(1, t))

    def partial_two(b):
        partial_rows(1, b)
        ng_copy(1, b, b).start()

    loop(BALLS, partial_two)
    early[:, : 3 * OWN] = dot(normed_t[1], dqkv[...]).astype(BF16)
    out_grad = dot(mix_t[1], g_all[1]).astype(BF16)
    early[:OWN, 3 * OWN : 4 * OWN] = out_grad[:, :OWN]
    early[OWN:, 3 * OWN : 4 * OWN] = out_grad[:, OWN:]

    def rows_two(b, total):
        ng_copy(1, b, b).wait()
        rows, gain_part = row_grads(1, b)
        x_all[2, rows_of(b)] = rows
        mine = ((b // 4) == c).astype(F32)
        return total + gain_part * mine

    gain_two_part = lax.fori_loop(0, BALLS, rows_two, jnp.zeros((1, D), F32), unroll=4)

    g_all[0] = dot(perm_t[...], x_all[2]).astype(BF16)
    out_grad = dot(mix_t[0], g_all[0]).astype(BF16)
    early[:OWN, 4 * OWN :] = out_grad[:, :OWN]
    early[OWN:, 4 * OWN :] = out_grad[:, OWN:]
    sum_early.scatter()
    loop(BALLS, lambda b: attend_back(0, b))
    loop(BALLS, lambda t: gather_parts(0, t))
    late[...] = dot(normed_t[0], dqkv[...]).astype(BF16)
    sum_late.scatter()

    def partial_one(j):
        partial_rows(0, other * 4 + j)
        ng_copy(0, other * 4 + j, j).start()

    loop(4, partial_one)
    loop(4, lambda j: partial_rows(0, c * 4 + j))
    sum_early.plane()

    def rows_one(j, total):
        ng_copy(0, other * 4 + j, j).wait()
        rows, gain_part = row_grads(0, c * 4 + j)
        points_grad[0, rows_of(j)] = rows
        return total + gain_part

    gain_one_part = lax.fori_loop(0, 4, rows_one, jnp.zeros((1, D), F32), unroll=4)
    near_gain[xy] = jnp.concatenate([gain_one_part, gain_two_part], axis=0)
    for copy in gain_first:
        copy.start()
    sum_late.plane()
    for copy in gain_first:
        copy.wait()
    deep_gain[z] = sum(near_gain[k] for k in range(near_count))
    for copy in gain_second:
        copy.start()
    sum_early.column()
    sum_late.column()
    for copy in gain_second:
        copy.wait()
    gain_sums[c] = sum(deep_gain[k] for k in range(planes))
    gain_across.start()
    sum_early.forward()
    sum_late.forward()
    sum_early.finish()
    sum_late.finish()
    gain_across.wait()


def spread_kernel(
    early,
    late,
    gain_sums,
    result_in,
    points_grad_in,
    result,
    points_grad,
    gain_one,
    qkv_one,
    out_one,
    gain_two,
    qkv_two,
    out_two,
):
    result[...] = result_in[...]
    points_grad[...] = points_grad_in[...]
    for core in range(2):
        here = slice(core * OWN, (core + 1) * OWN)
        for n in range(3):
            into = slice(n * D + core * OWN, n * D + (core + 1) * OWN)
            qkv_one[:, into] = late[core, :, n * OWN : (n + 1) * OWN].astype(F32)
            qkv_two[:, into] = early[core, :, n * OWN : (n + 1) * OWN].astype(F32)
        for at, out in ((4 * OWN, out_one), (3 * OWN, out_two)):
            out[here, :OWN] = early[core, :OWN, at : at + OWN].astype(F32)
            out[here, OWN:] = early[core, OWN:, at : at + OWN].astype(F32)
    gains = gain_sums[0] + gain_sums[1]
    gain_one[...] = gains[0]
    gain_two[...] = gains[1]


def vmem():
    return pl.BlockSpec(memory_space=pltpu.VMEM)


def hbm():
    return pl.BlockSpec(memory_space=pltpu.HBM)


def layers_call(near_count, planes, *args):
    chunk = D // near_count
    peers = max(near_count - 1, 1)
    deeper = max(planes - 1, 1)
    return pl.pallas_call(
        functools.partial(layers_kernel, near_count, planes),
        name="layers",
        out_shape=(
            jax.ShapeDtypeStruct((1, HALF, D), BF16),
            jax.ShapeDtypeStruct((1, HALF, D), BF16),
            jax.ShapeDtypeStruct((2, D, 5 * OWN), BF16),
            jax.ShapeDtypeStruct((2, D, 3 * OWN), BF16),
            jax.ShapeDtypeStruct((2, 2, D), F32),
        ),
        in_specs=[hbm()] * 5 + [vmem(), hbm(), hbm()] * 2,
        out_specs=(vmem(),) * 5,
        scratch_shapes=[
            pltpu.VMEM((3, ROWS, D), BF16),
            pltpu.VMEM((2, ROWS, D), BF16),
            pltpu.VMEM((2, 2, 4, LISTED), jnp.int32),
            pltpu.SMEM((2, 2, 4, LISTED), jnp.int32),
            pltpu.VMEM((2, 1, HALF), jnp.int32),
            pltpu.VMEM((2, D, 3 * OWN), BF16),
            pltpu.VMEM((2, D, D), BF16),
            pltpu.VMEM((2, D, ROWS), BF16),
            pltpu.VMEM((2, BALLS, 2 * BALL, OWN), BF16),
            pltpu.VMEM((2, BALLS, BALL, 2 * OWN), BF16),
            pltpu.VMEM((2, BALLS, OWN, BALL), BF16),
            pltpu.VMEM((2, BALLS, OWN, BALL), BF16),
            pltpu.VMEM((2, BALLS, LISTED * BALL, 2 * BALL), F32),
            pltpu.VMEM((2, OWN, ROWS), BF16),
            pltpu.VMEM((2, 2, ROWS, OWN), BF16),
            pltpu.VMEM((ROWS, 3 * OWN), BF16),
            pltpu.VMEM((LISTED * BALLS + 1, BALL, D), F32),
            pltpu.VMEM((2, 2, ROWS, D), BF16),
            pltpu.VMEM((ROWS, ROWS), BF16),
            pltpu.VMEM((ROWS, ROWS), BF16),
            pltpu.VMEM((D, 5 * OWN), BF16),
            pltpu.VMEM((D, 3 * OWN), BF16),
            pltpu.VMEM((peers, chunk, 5 * OWN), BF16),
            pltpu.VMEM((peers, chunk, 3 * OWN), BF16),
            pltpu.VMEM((planes, chunk, 5 * OWN), BF16),
            pltpu.VMEM((planes, chunk, 3 * OWN), BF16),
            pltpu.VMEM((near_count, 2, D), F32),
            pltpu.VMEM((planes, 2, D), F32),
            pltpu.SemaphoreType.DMA((5,)),
            pltpu.SemaphoreType.DMA((5,)),
            pltpu.SemaphoreType.DMA((5,)),
            pltpu.SemaphoreType.DMA((8,)),
            pltpu.SemaphoreType.DMA,
            pltpu.SemaphoreType.DMA((2, BALLS)),
            pltpu.SemaphoreType.DMA((2, BALLS)),
            pltpu.SemaphoreType.DMA((2, BALLS)),
            pltpu.SemaphoreType.DMA((2, BALLS)),
            pltpu.SemaphoreType.DMA((3, peers)),
            pltpu.SemaphoreType.DMA((3, peers)),
            pltpu.SemaphoreType.DMA((3, deeper)),
            pltpu.SemaphoreType.DMA((3, deeper)),
            pltpu.SemaphoreType.DMA((2, peers)),
            pltpu.SemaphoreType.DMA((2, peers)),
            pltpu.SemaphoreType.DMA((3, near_count)),
            pltpu.SemaphoreType.DMA((3, near_count)),
        ],
        compiler_params=pltpu.CompilerParams(
            collective_id=0, has_side_effects=True, vmem_limit_bytes=56 << 20
        ),
    )(*args)


def spread_call(early, late, gain_sums, result, points_grad):
    shapes = (
        jax.ShapeDtypeStruct((D,), F32),
        jax.ShapeDtypeStruct((D, 3 * D), F32),
        jax.ShapeDtypeStruct((D, D), F32),
    )
    rows = jax.ShapeDtypeStruct((1, HALF, D), BF16)
    return pl.pallas_call(
        spread_kernel,
        name="spread",
        out_shape=(rows, rows) + shapes + shapes,
        in_specs=[vmem()] * 5,
        out_specs=(vmem(),) * 8,
    )(early, late, gain_sums, result, points_grad)


def local(*args):
    planes = lax.axis_size("geo") // XY
    result, points_grad, early, late, gain_sums = layers_call(XY, planes, *args)
    return spread_call(early, late, gain_sums, result, points_grad)


def solution(mesh):
    rows = P("geo", "pts", None)
    placed = (rows, rows, rows, rows, P("geo", "pts"), P(), P(), P(), P(), P(), P())
    return jax.shard_map(
        local,
        mesh=mesh,
        in_specs=placed,
        out_specs=(rows, rows, P(), P(), P(), P(), P(), P()),
        check_vma=False,
    )
```

```python
import functools

import jax
import jax.numpy as jnp
from jax import lax
from jax.experimental import pallas as pl
from jax.experimental.pallas import tpu as pltpu
from jax.sharding import PartitionSpec as P

HEADS = 4
BALL = 128
LISTED = 4
BALLS = 8
ROWS = BALL * BALLS
HALF = ROWS // 2
D = 256
OWN = 128
EPSILON = 1e-06
XY = 16
MESH = pl.DeviceIdType.MESH
F32 = jnp.float32
BF16 = jnp.bfloat16


def dot(a, b):
    return jnp.dot(a, b, preferred_element_type=F32)


def dot_nt(a, b):
    return lax.dot_general(a, b, (((1,), (1,)), ((), ())), preferred_element_type=F32)


def rows_of(b, size=BALL):
    return pl.ds(pl.multiple_of(b * size, size), size)


def layers_kernel(
    near_count,
    planes,
    points,
    result_grad,
    lists_one,
    lists_two,
    rotation,
    gain_one,
    qkv_one,
    out_one,
    gain_two,
    qkv_two,
    out_two,
    result,
    points_grad,
    full_early,
    full_third,
    full_late,
    gain_sums,
    x_all,
    g_all,
    lists_v,
    lists_s,
    rot_v,
    w_own,
    w_out,
    normed_t,
    q_st,
    kv_all,
    k_t,
    v_t,
    att,
    mix_t,
    mix_f,
    mixed,
    dqkv,
    parts,
    ngrad,
    perm,
    perm_t,
    early,
    third,
    late,
    near_early,
    near_third,
    near_late,
    deep_early,
    deep_third,
    deep_late,
    near_gain,
    deep_gain,
    in_send,
    in_recv,
    own_sem,
    load_sem,
    smem_sem,
    mix_send,
    mix_recv,
    ng_send,
    ng_recv,
    send_xy,
    recv_xy,
    send_z,
    recv_z,
    send_all,
    recv_all,
    send_core,
    recv_core,
):
    c = lax.axis_index("pts")
    other = 1 - c
    geo = lax.axis_index("geo")
    z = geo // near_count
    xy = geo % near_count
    chunk = D // near_count
    gains = (gain_one, gain_two)
    qkvs = (qkv_one, qkv_two)
    outs = (out_one, out_two)

    def copy_to(device, src, dst, send, recv):
        return pltpu.make_async_remote_copy(
            src_ref=src,
            dst_ref=dst,
            send_sem=send,
            recv_sem=recv,
            device_id=device,
            device_id_type=MESH,
        )

    def remote(src, dst, send, recv):
        return copy_to({"pts": other}, src, dst, send, recv)

    def near(k):
        return {"geo": z * near_count + (xy + k) % near_count}

    def deep(k):
        return {"geo": ((z + k) % planes) * near_count + xy}

    barrier = pltpu.get_barrier_semaphore()
    pl.semaphore_signal(barrier, inc=1, device_id={"pts": other}, device_id_type=MESH)
    for k in range(1, near_count):
        pl.semaphore_signal(barrier, inc=1, device_id=near(k), device_id_type=MESH)
    for k in range(1, planes):
        pl.semaphore_signal(barrier, inc=1, device_id=deep(k), device_id_type=MESH)

    inputs = (
        (points.at[0], x_all.at[0, rows_of(c, HALF)]),
        (lists_one.at[0], lists_v.at[0, c]),
        (lists_two.at[0], lists_v.at[1, c]),
        (rotation, rot_v.at[c]),
        (result_grad.at[0], g_all.at[1, rows_of(c, HALF)]),
    )
    kept = [
        pltpu.make_async_copy(src, dst, own_sem.at[n]) for n, (src, dst) in enumerate(inputs)
    ]
    sent = [
        remote(src, dst, in_send.at[n], in_recv.at[n]) for n, (src, dst) in enumerate(inputs)
    ]
    loads = []
    for i in range(2):
        for n in range(3):
            part = pl.ds(pl.multiple_of(n * D + c * OWN, OWN), OWN)
            loads.append(
                pltpu.make_async_copy(
                    qkvs[i].at[:, part],
                    w_own.at[i, :, n * OWN : (n + 1) * OWN],
                    load_sem.at[4 * i + n],
                )
            )
        loads.append(pltpu.make_async_copy(outs[i], w_out.at[i], load_sem.at[4 * i + 3]))
    kept[0].start()
    for copy in loads[:3]:
        copy.start()
    for copy in kept[1:] + loads[3:]:
        copy.start()
    parts[LISTED * BALLS] = jnp.zeros((BALL, D), F32)
    col = pl.ds(pl.multiple_of(c * OWN, OWN), OWN)

    lane = lax.broadcasted_iota(jnp.int32, (BALL, OWN), 1)
    first = lane < OWN // 2

    def stacked(value):
        zero = jnp.zeros_like(value)
        return jnp.concatenate(
            [jnp.where(first, value, zero), jnp.where(first, zero, value)], axis=0
        )

    def unstacked_t(value):
        return jnp.concatenate([value[: OWN // 2, :BALL], value[OWN // 2 :, BALL:]], axis=0)

    def project(i, b):
        x = x_all[i, rows_of(b)].astype(F32)
        gain = gains[i][...].astype(F32).reshape(1, D)
        factor = lax.rsqrt(jnp.mean(x * x, axis=-1, keepdims=True) + EPSILON)
        normed = x * factor * gain
        normed_t[i, :, rows_of(b)] = normed.T.astype(BF16)
        qkv = dot(normed.astype(BF16), w_own[i])
        q = qkv[:, :OWN].astype(BF16).astype(F32) * 0.125
        q_st[i, b] = stacked(q).astype(BF16)
        kv_all[i, b] = qkv[:, OWN:].astype(BF16)
        k_t[i, b] = qkv[:, OWN : 2 * OWN].T.astype(BF16)
        v_t[i, b] = qkv[:, 2 * OWN :].T.astype(BF16)

    def listed(i, b):
        return [lists_s[i, b // 4, b % 4, n] for n in range(LISTED)]

    def attend(i, b):
        ids = listed(i, b)
        queries = q_st[i, b]
        scores = [dot_nt(kv_all[i, t, :, :OWN], queries) for t in ids]
        top = jnp.maximum(jnp.maximum(scores[0], scores[1]), jnp.maximum(scores[2], scores[3]))
        top = jnp.max(top, axis=0, keepdims=True)
        exponents = [jnp.exp(score - top) for score in scores]
        total = (exponents[0] + exponents[1]) + (exponents[2] + exponents[3])
        scale = 1.0 / jnp.sum(total, axis=0, keepdims=True)
        weights = [(exponent * scale).astype(BF16) for exponent in exponents]
        for n in range(LISTED):
            att[i, b, n * BALL : (n + 1) * BALL] = weights[n]
        values_t = jnp.concatenate([v_t[i, t] for t in ids], axis=1)
        own_t = unstacked_t(dot(values_t, jnp.concatenate(weights, axis=0)))
        mix_f[i, :, rows_of(b)] = own_t
        mix_t[i, :, rows_of(b)] = own_t.astype(BF16)
        mixed[i, c, rows_of(b)] = own_t.T.astype(BF16)

    def loop(count, body, unroll=4):
        lax.fori_loop(0, count, lambda j, _: body(j), None, unroll=unroll)

    def mix_copy(i, b, slot):
        ref = mixed.at[i, c, rows_of(b)]
        return remote(ref, ref, mix_send.at[i, slot], mix_recv.at[i, slot])

    def project_out(i, b):
        both = jnp.concatenate([mixed[i, 0, rows_of(b)], mixed[i, 1, rows_of(b)]], axis=1)
        x = x_all[i, rows_of(b)].astype(F32)
        return (x + dot(both, w_out[i])).astype(BF16)

    def build(b):
        here = rot_v[b // 4, :, rows_of(b % 4)].astype(F32)
        column = jnp.broadcast_to(here, (BALL, BALL)).T
        for n in range(BALLS):
            ids = (lane + n * BALL).astype(F32)
            perm[rows_of(b), n * BALL : (n + 1) * BALL] = jnp.where(
                ids == column, 1.0, 0.0
            ).astype(BF16)

    def build_t(b):
        ids = lax.broadcasted_iota(jnp.int32, (BALL, ROWS), 0) + b * BALL
        rot_row = jnp.concatenate([rot_v[0], rot_v[1]], axis=1)
        perm_t[rows_of(b)] = jnp.where(ids == rot_row, 1.0, 0.0).astype(BF16)

    kept[0].wait()
    for copy in loads[:3]:
        copy.wait()
    loop(4, lambda j: project(0, c * 4 + j))
    for copy in kept[1:4]:
        copy.wait()
    loop(4, lambda j: build(c * 4 + j))
    pl.semaphore_wait(barrier, near_count + planes - 1)
    for copy in sent:
        copy.start()
    for n in (1, 2, 3):
        sent[n].wait()
    to_smem = pltpu.make_async_copy(lists_v, lists_s, smem_sem)
    to_smem.start()
    sent[0].wait()
    loop(4, lambda j: project(0, other * 4 + j))
    to_smem.wait()
    for copy in loads[3:]:
        copy.wait()

    def attend_send(j):
        attend(0, j)
        mix_copy(0, j, j).start()

    loop(BALLS, attend_send)
    loop(BALLS, build_t)
    loop(4, lambda j: build(other * 4 + j))

    def hidden_rows(b):
        mix_copy(0, b, b).wait()
        x_all[2, rows_of(b)] = project_out(0, b)

    loop(BALLS, hidden_rows)
    x_all[1] = dot(perm[...], x_all[2]).astype(BF16)
    loop(BALLS, lambda b: project(1, b))

    def attend_two(j):
        attend(1, other * 4 + j)
        mix_copy(1, other * 4 + j, j).start()

    loop(4, attend_two)
    loop(4, lambda j: attend(1, c * 4 + j))

    def result_rows(j):
        mix_copy(1, other * 4 + j, j).wait()
        result[0, rows_of(j)] = project_out(1, c * 4 + j)

    kept[4].wait()
    sent[4].wait()

    def attend_back(i, b):
        ids = listed(i, b)
        grads = g_all[i, rows_of(b)]
        own_out = w_out[i, col, :]
        mixed_grad = stacked(dot_nt(grads, own_out)).astype(BF16)
        mixed_grad_t = dot_nt(own_out, grads).astype(BF16).astype(F32)
        product = mixed_grad_t * mix_f[i, :, rows_of(b)]
        half = OWN // 2
        inner = jnp.concatenate(
            [
                jnp.sum(product[:half], axis=0, keepdims=True),
                jnp.sum(product[half:], axis=0, keepdims=True),
            ],
            axis=1,
        )
        values = jnp.concatenate([kv_all[i, t, :, OWN:] for t in ids], axis=0)
        weights = att[i, b]
        scores_grad = jnp.concatenate(
            [
                (
                    weights[:, cols].astype(F32)
                    * (dot_nt(values, mixed_grad[cols]) - inner[:, cols])
                ).astype(BF16)
                for cols in (slice(0, BALL), slice(BALL, 2 * BALL))
            ],
            axis=1,
        )
        values_grad = dot(weights, mixed_grad)
        keys_grad = dot(scores_grad, q_st[i, b])
        for n in range(LISTED):
            parts[b * LISTED + n, :, :OWN] = keys_grad[n * BALL : (n + 1) * BALL]
            parts[b * LISTED + n, :, OWN:] = values_grad[n * BALL : (n + 1) * BALL]
        keys_t = jnp.concatenate([k_t[i, t] for t in ids], axis=1)
        query_grad_t = unstacked_t(dot(keys_t, scores_grad)) * 0.125
        dqkv[rows_of(b), :OWN] = query_grad_t.T.astype(BF16)

    def gather_parts(i, t):
        total = jnp.zeros((BALL, D), F32)
        for b in range(BALLS):
            at = jnp.int32(LISTED * BALLS)
            for n in range(LISTED):
                at = jnp.where(lists_s[i, b // 4, b % 4, n] == t, b * LISTED + n, at)
            total = total + parts[at]
        dqkv[rows_of(t), OWN:] = total.astype(BF16)

    def ng_copy(i, b, slot):
        ref = ngrad.at[i, c, rows_of(b)]
        return remote(ref, ref, ng_send.at[i, slot], ng_recv.at[i, slot])

    def partial_rows(i, b):
        ngrad[i, c, rows_of(b)] = dot_nt(dqkv[rows_of(b)], w_own[i]).astype(BF16)

    def row_grads(i, b):
        x = x_all[i, rows_of(b)].astype(F32)
        gain = gains[i][...].astype(F32).reshape(1, D)
        factor = lax.rsqrt(jnp.mean(x * x, axis=-1, keepdims=True) + EPSILON)
        grad = ngrad[i, 0, rows_of(b)].astype(F32) + ngrad[i, 1, rows_of(b)].astype(F32)
        grad = grad.astype(BF16).astype(F32)
        scaled = grad * gain
        inner = jnp.mean(scaled * x, axis=-1, keepdims=True)
        inputs_grad = factor * scaled - x * (factor * factor * factor) * inner
        rows = (g_all[i, rows_of(b)].astype(F32) + inputs_grad).astype(BF16)
        return rows, jnp.sum(grad * (x * factor), axis=0, keepdims=True)

    class Sum:
        def __init__(self, r, groups, own, arrived, along, full):
            self.r, self.own, self.arrived, self.along, self.full = r, own, arrived, along, full
            at = rows_of(xy, chunk)
            self.first = [
                [
                    copy_to(
                        near(k),
                        own.at[rows_of((xy + k) % near_count, chunk), cols],
                        arrived.at[k - 1, :, cols],
                        send_xy.at[r + m, k - 1],
                        recv_xy.at[r + m, k - 1],
                    )
                    for k in range(1, near_count)
                ]
                for m, cols in enumerate(groups)
            ]
            self.second = [
                copy_to(
                    deep(k), along.at[z], along.at[z], send_z.at[r, k - 1], recv_z.at[r, k - 1]
                )
                for k in range(1, planes)
            ]
            mine = full.at[c, at]
            self.third = [
                copy_to(near(k), mine, mine, send_all.at[r, k - 1], recv_all.at[r, k - 1])
                for k in range(1, near_count)
            ]
            pieces = [
                full.at[c, rows_of((xy - k + near_count) % near_count, chunk)]
                for k in range(near_count)
            ]
            self.across = [
                remote(piece, piece, send_core.at[r, k], recv_core.at[r, k])
                for k, piece in enumerate(pieces)
            ]

        def scatter(self, m=0):
            for copy in self.first[m]:
                copy.start()

        def plane(self):
            total = self.own[rows_of(xy, chunk)].astype(F32)
            for k in range(near_count - 1):
                for group in self.first:
                    group[k].wait()
                total = total + self.arrived[k].astype(F32)
            self.along[z] = total.astype(BF16)
            for copy in self.second:
                copy.start()

        def column(self):
            for copy in self.second:
                copy.wait()
            total = self.along[0].astype(F32)
            for k in range(1, planes):
                total = total + self.along[k].astype(F32)
            self.full[c, rows_of(xy, chunk)] = total.astype(BF16)
            for copy in self.third:
                copy.start()
            self.across[0].start()

        def forward(self):
            for k, copy in enumerate(self.third):
                copy.wait_recv()
                self.across[k + 1].start()

        def finish(self):
            for copy in self.third:
                copy.wait_send()
            for copy in self.across:
                copy.wait()

    out_cols, in_cols = slice(3 * OWN, 4 * OWN), slice(0, 3 * OWN)
    sum_early = Sum(0, (out_cols, in_cols), early, near_early, deep_early, full_early)
    sum_third = Sum(2, (slice(0, OWN),), third, near_third, deep_third, full_third)
    sum_late = Sum(3, (in_cols,), late, near_late, deep_late, full_late)
    gain_first = [
        copy_to(
            near(k), near_gain.at[xy], near_gain.at[xy], send_xy.at[4, k - 1], recv_xy.at[4, k - 1]
        )
        for k in range(1, near_count)
    ]
    gain_second = [
        copy_to(deep(k), deep_gain.at[z], deep_gain.at[z], send_z.at[4, k - 1], recv_z.at[4, k - 1])
        for k in range(1, planes)
    ]
    gain_across = remote(
        gain_sums.at[c], gain_sums.at[c], send_core.at[4, 0], recv_core.at[4, 0]
    )

    def pack_out(i, into, at):
        out_grad = dot(mix_t[i], g_all[i]).astype(BF16)
        into[:OWN, at : at + OWN] = out_grad[:, :OWN]
        into[OWN:, at : at + OWN] = out_grad[:, OWN:]

    pack_out(1, early, 3 * OWN)
    sum_early.scatter(0)
    loop(BALLS, lambda b: attend_back(1, b))
    loop(BALLS, lambda t: gather_parts(1, t))

    def partial_two(b):
        partial_rows(1, b)
        ng_copy(1, b, b).start()

    loop(BALLS, partial_two)
    early[:, : 3 * OWN] = dot(normed_t[1], dqkv[...]).astype(BF16)
    sum_early.scatter(1)

    def rows_two(b, total):
        ng_copy(1, b, b).wait()
        rows, gain_part = row_grads(1, b)
        x_all[2, rows_of(b)] = rows
        mine = ((b // 4) == c).astype(F32)
        return total + gain_part * mine

    gain_two_part = lax.fori_loop(0, BALLS, rows_two, jnp.zeros((1, D), F32), unroll=4)

    g_all[0] = dot(perm_t[...], x_all[2]).astype(BF16)
    pack_out(0, third, 0)
    sum_third.scatter()
    loop(4, lambda b: attend_back(0, b))
    sum_early.plane()
    loop(4, lambda b: attend_back(0, b + 4))
    loop(BALLS, lambda t: gather_parts(0, t))
    late[...] = dot(normed_t[0], dqkv[...]).astype(BF16)
    sum_late.scatter()
    sum_third.plane()

    def partial_one(j):
        partial_rows(0, other * 4 + j)
        ng_copy(0, other * 4 + j, j).start()

    loop(4, partial_one)
    loop(4, lambda j: partial_rows(0, c * 4 + j))

    def rows_one(j, total):
        ng_copy(0, other * 4 + j, j).wait()
        rows, gain_part = row_grads(0, c * 4 + j)
        points_grad[0, rows_of(j)] = rows
        return total + gain_part

    gain_one_part = lax.fori_loop(0, 4, rows_one, jnp.zeros((1, D), F32), unroll=4)
    near_gain[xy] = jnp.concatenate([gain_one_part, gain_two_part], axis=0)
    for copy in gain_first:
        copy.start()
    sum_early.column()
    sum_late.plane()
    sum_third.column()
    for copy in gain_first:
        copy.wait()
    deep_gain[z] = sum(near_gain[k] for k in range(near_count))
    for copy in gain_second:
        copy.start()
    loop(4, result_rows)
    sum_late.column()
    for copy in gain_second:
        copy.wait()
    gain_sums[c] = sum(deep_gain[k] for k in range(planes))
    gain_across.start()
    sums = (sum_early, sum_third, sum_late)
    for item in sums:
        item.forward()
    for item in sums:
        item.finish()
    gain_across.wait()


def spread_kernel(
    early,
    third,
    late,
    gain_sums,
    result_in,
    points_grad_in,
    result,
    points_grad,
    gain_one,
    qkv_one,
    out_one,
    gain_two,
    qkv_two,
    out_two,
):
    result[...] = result_in[...]
    points_grad[...] = points_grad_in[...]
    for core in range(2):
        here = slice(core * OWN, (core + 1) * OWN)
        for n in range(3):
            into = slice(n * D + core * OWN, n * D + (core + 1) * OWN)
            qkv_one[:, into] = late[core, :, n * OWN : (n + 1) * OWN].astype(F32)
            qkv_two[:, into] = early[core, :, n * OWN : (n + 1) * OWN].astype(F32)
        for at, of, out in ((0, third, out_one), (3 * OWN, early, out_two)):
            out[here, :OWN] = of[core, :OWN, at : at + OWN].astype(F32)
            out[here, OWN:] = of[core, OWN:, at : at + OWN].astype(F32)
    gains = gain_sums[0] + gain_sums[1]
    gain_one[...] = gains[0]
    gain_two[...] = gains[1]


def vmem():
    return pl.BlockSpec(memory_space=pltpu.VMEM)


def hbm():
    return pl.BlockSpec(memory_space=pltpu.HBM)


def layers_call(near_count, planes, *args):
    chunk = D // near_count
    peers = max(near_count - 1, 1)
    deeper = max(planes - 1, 1)
    return pl.pallas_call(
        functools.partial(layers_kernel, near_count, planes),
        name="layers",
        out_shape=(
            jax.ShapeDtypeStruct((1, HALF, D), BF16),
            jax.ShapeDtypeStruct((1, HALF, D), BF16),
            jax.ShapeDtypeStruct((2, D, 4 * OWN), BF16),
            jax.ShapeDtypeStruct((2, D, OWN), BF16),
            jax.ShapeDtypeStruct((2, D, 3 * OWN), BF16),
            jax.ShapeDtypeStruct((2, 2, D), F32),
        ),
        in_specs=[hbm()] * 5 + [vmem(), hbm(), hbm()] * 2,
        out_specs=(vmem(),) * 6,
        scratch_shapes=[
            pltpu.VMEM((3, ROWS, D), BF16),
            pltpu.VMEM((2, ROWS, D), BF16),
            pltpu.VMEM((2, 2, 4, LISTED), jnp.int32),
            pltpu.SMEM((2, 2, 4, LISTED), jnp.int32),
            pltpu.VMEM((2, 1, HALF), jnp.int32),
            pltpu.VMEM((2, D, 3 * OWN), BF16),
            pltpu.VMEM((2, D, D), BF16),
            pltpu.VMEM((2, D, ROWS), BF16),
            pltpu.VMEM((2, BALLS, 2 * BALL, OWN), BF16),
            pltpu.VMEM((2, BALLS, BALL, 2 * OWN), BF16),
            pltpu.VMEM((2, BALLS, OWN, BALL), BF16),
            pltpu.VMEM((2, BALLS, OWN, BALL), BF16),
            pltpu.VMEM((2, BALLS, LISTED * BALL, 2 * BALL), BF16),
            pltpu.VMEM((2, OWN, ROWS), BF16),
            pltpu.VMEM((2, OWN, ROWS), F32),
            pltpu.VMEM((2, 2, ROWS, OWN), BF16),
            pltpu.VMEM((ROWS, 3 * OWN), BF16),
            pltpu.VMEM((LISTED * BALLS + 1, BALL, D), F32),
            pltpu.VMEM((2, 2, ROWS, D), BF16),
            pltpu.VMEM((ROWS, ROWS), BF16),
            pltpu.VMEM((ROWS, ROWS), BF16),
            pltpu.VMEM((D, 4 * OWN), BF16),
            pltpu.VMEM((D, OWN), BF16),
            pltpu.VMEM((D, 3 * OWN), BF16),
            pltpu.VMEM((peers, chunk, 4 * OWN), BF16),
            pltpu.VMEM((peers, chunk, OWN), BF16),
            pltpu.VMEM((peers, chunk, 3 * OWN), BF16),
            pltpu.VMEM((planes, chunk, 4 * OWN), BF16),
            pltpu.VMEM((planes, chunk, OWN), BF16),
            pltpu.VMEM((planes, chunk, 3 * OWN), BF16),
            pltpu.VMEM((near_count, 2, D), F32),
            pltpu.VMEM((planes, 2, D), F32),
            pltpu.SemaphoreType.DMA((5,)),
            pltpu.SemaphoreType.DMA((5,)),
            pltpu.SemaphoreType.DMA((5,)),
            pltpu.SemaphoreType.DMA((8,)),
            pltpu.SemaphoreType.DMA,
            pltpu.SemaphoreType.DMA((2, BALLS)),
            pltpu.SemaphoreType.DMA((2, BALLS)),
            pltpu.SemaphoreType.DMA((2, BALLS)),
            pltpu.SemaphoreType.DMA((2, BALLS)),
            pltpu.SemaphoreType.DMA((5, peers)),
            pltpu.SemaphoreType.DMA((5, peers)),
            pltpu.SemaphoreType.DMA((5, deeper)),
            pltpu.SemaphoreType.DMA((5, deeper)),
            pltpu.SemaphoreType.DMA((4, peers)),
            pltpu.SemaphoreType.DMA((4, peers)),
            pltpu.SemaphoreType.DMA((5, near_count)),
            pltpu.SemaphoreType.DMA((5, near_count)),
        ],
        compiler_params=pltpu.CompilerParams(
            collective_id=0, has_side_effects=True, vmem_limit_bytes=56 << 20
        ),
    )(*args)


def spread_call(*args):
    shapes = (
        jax.ShapeDtypeStruct((D,), F32),
        jax.ShapeDtypeStruct((D, 3 * D), F32),
        jax.ShapeDtypeStruct((D, D), F32),
    )
    rows = jax.ShapeDtypeStruct((1, HALF, D), BF16)
    return pl.pallas_call(
        spread_kernel,
        name="spread",
        out_shape=(rows, rows) + shapes + shapes,
        in_specs=[vmem()] * 6,
        out_specs=(vmem(),) * 8,
        compiler_params=pltpu.CompilerParams(vmem_limit_bytes=16 << 20),
    )(*args)


def local(*args):
    planes = lax.axis_size("geo") // XY
    result, points_grad, *sums = layers_call(XY, planes, *args)
    return spread_call(*sums, result, points_grad)


def solution(mesh):
    rows = P("geo", "pts", None)
    placed = (rows, rows, rows, rows, P("geo", "pts"), P(), P(), P(), P(), P(), P())
    return jax.shard_map(
        local,
        mesh=mesh,
        in_specs=placed,
        out_specs=(rows, rows, P(), P(), P(), P(), P(), P()),
        check_vma=False,
    )
```

```python
import functools

import jax
import jax.numpy as jnp
from jax import lax
from jax.experimental import pallas as pl
from jax.experimental.pallas import tpu as pltpu
from jax.sharding import PartitionSpec as P

HEADS = 4
BALL = 128
LISTED = 4
BALLS = 8
ROWS = BALL * BALLS
HALF = ROWS // 2
D = 256
OWN = 128
EPSILON = 1e-06
XY = 16
MESH = pl.DeviceIdType.MESH
F32 = jnp.float32
BF16 = jnp.bfloat16


def dot(a, b):
    return jnp.dot(a, b, preferred_element_type=F32)


def dot_nt(a, b):
    return lax.dot_general(a, b, (((1,), (1,)), ((), ())), preferred_element_type=F32)


def rows_of(b, size=BALL):
    return pl.ds(pl.multiple_of(b * size, size), size)


def layers_kernel(
    near_count,
    planes,
    points,
    result_grad,
    lists_one,
    lists_two,
    rotation,
    gain_one,
    qkv_one,
    out_one,
    gain_two,
    qkv_two,
    out_two,
    result,
    points_grad,
    full_early,
    full_late,
    gain_sums,
    x_all,
    g_all,
    lists_v,
    lists_s,
    rot_v,
    w_own,
    w_out,
    normed_t,
    q_st,
    kv_all,
    k_t,
    v_t,
    att,
    mix_t,
    mix_f,
    mixed,
    dqkv,
    parts,
    ngrad,
    perm,
    perm_t,
    early,
    late,
    near_early,
    near_late,
    deep_early,
    deep_late,
    near_gain,
    deep_gain,
    in_send,
    in_recv,
    own_sem,
    load_sem,
    smem_sem,
    mix_send,
    mix_recv,
    ng_send,
    ng_recv,
    send_xy,
    recv_xy,
    send_z,
    recv_z,
    send_all,
    recv_all,
    send_core,
    recv_core,
):
    c = lax.axis_index("pts")
    other = 1 - c
    geo = lax.axis_index("geo")
    z = geo // near_count
    xy = geo % near_count
    chunk = D // near_count
    gains = (gain_one, gain_two)
    qkvs = (qkv_one, qkv_two)
    outs = (out_one, out_two)

    def copy_to(device, src, dst, send, recv):
        return pltpu.make_async_remote_copy(
            src_ref=src,
            dst_ref=dst,
            send_sem=send,
            recv_sem=recv,
            device_id=device,
            device_id_type=MESH,
        )

    def remote(src, dst, send, recv):
        return copy_to({"pts": other}, src, dst, send, recv)

    def near(k):
        return {"geo": z * near_count + (xy + k) % near_count}

    def deep(k):
        return {"geo": ((z + k) % planes) * near_count + xy}

    barrier = pltpu.get_barrier_semaphore()
    pl.semaphore_signal(barrier, inc=1, device_id={"pts": other}, device_id_type=MESH)
    for k in range(1, near_count):
        pl.semaphore_signal(barrier, inc=1, device_id=near(k), device_id_type=MESH)
    for k in range(1, planes):
        pl.semaphore_signal(barrier, inc=1, device_id=deep(k), device_id_type=MESH)

    inputs = (
        (points.at[0], x_all.at[0, rows_of(c, HALF)]),
        (lists_one.at[0], lists_v.at[0, c]),
        (lists_two.at[0], lists_v.at[1, c]),
        (rotation, rot_v.at[c]),
        (result_grad.at[0], g_all.at[1, rows_of(c, HALF)]),
    )
    kept = [
        pltpu.make_async_copy(src, dst, own_sem.at[n]) for n, (src, dst) in enumerate(inputs)
    ]
    sent = [
        remote(src, dst, in_send.at[n], in_recv.at[n]) for n, (src, dst) in enumerate(inputs)
    ]
    loads = []
    for i in range(2):
        for n in range(3):
            part = pl.ds(pl.multiple_of(n * D + c * OWN, OWN), OWN)
            loads.append(
                pltpu.make_async_copy(
                    qkvs[i].at[:, part],
                    w_own.at[i, :, n * OWN : (n + 1) * OWN],
                    load_sem.at[4 * i + n],
                )
            )
        loads.append(pltpu.make_async_copy(outs[i], w_out.at[i], load_sem.at[4 * i + 3]))
    kept[0].start()
    for copy in loads[:3]:
        copy.start()
    for copy in kept[1:] + loads[3:]:
        copy.start()
    parts[LISTED * BALLS] = jnp.zeros((BALL, D), F32)
    col = pl.ds(pl.multiple_of(c * OWN, OWN), OWN)

    lane = lax.broadcasted_iota(jnp.int32, (BALL, OWN), 1)
    first = lane < OWN // 2

    def stacked(value):
        zero = jnp.zeros_like(value)
        return jnp.concatenate(
            [jnp.where(first, value, zero), jnp.where(first, zero, value)], axis=0
        )

    def unstacked_t(value):
        return jnp.concatenate([value[: OWN // 2, :BALL], value[OWN // 2 :, BALL:]], axis=0)

    def project(i, b):
        x = x_all[i, rows_of(b)].astype(F32)
        gain = gains[i][...].astype(F32).reshape(1, D)
        factor = lax.rsqrt(jnp.mean(x * x, axis=-1, keepdims=True) + EPSILON)
        normed = x * factor * gain
        normed_t[i, :, rows_of(b)] = normed.T.astype(BF16)
        qkv = dot(normed.astype(BF16), w_own[i])
        q = qkv[:, :OWN].astype(BF16).astype(F32) * 0.125
        q_st[i, b] = stacked(q).astype(BF16)
        kv_all[i, b] = qkv[:, OWN:].astype(BF16)
        k_t[i, b] = qkv[:, OWN : 2 * OWN].T.astype(BF16)
        v_t[i, b] = qkv[:, 2 * OWN :].T.astype(BF16)

    def listed(i, b):
        return [lists_s[i, b // 4, b % 4, n] for n in range(LISTED)]

    def attend(i, b):
        ids = listed(i, b)
        queries = q_st[i, b]
        scores = [dot_nt(kv_all[i, t, :, :OWN], queries) for t in ids]
        top = jnp.maximum(jnp.maximum(scores[0], scores[1]), jnp.maximum(scores[2], scores[3]))
        top = jnp.max(top, axis=0, keepdims=True)
        exponents = [jnp.exp(score - top) for score in scores]
        total = (exponents[0] + exponents[1]) + (exponents[2] + exponents[3])
        scale = 1.0 / jnp.sum(total, axis=0, keepdims=True)
        weights = [(exponent * scale).astype(BF16) for exponent in exponents]
        for n in range(LISTED):
            att[i, b, n * BALL : (n + 1) * BALL] = weights[n]
        values_t = jnp.concatenate([v_t[i, t] for t in ids], axis=1)
        own_t = unstacked_t(dot(values_t, jnp.concatenate(weights, axis=0)))
        mix_f[i, :, rows_of(b)] = own_t
        mix_t[i, :, rows_of(b)] = own_t.astype(BF16)
        mixed[i, c, rows_of(b)] = own_t.T.astype(BF16)

    def loop(count, body, unroll=4):
        lax.fori_loop(0, count, lambda j, _: body(j), None, unroll=unroll)

    def mix_copy(i, b, slot):
        ref = mixed.at[i, c, rows_of(b)]
        return remote(ref, ref, mix_send.at[i, slot], mix_recv.at[i, slot])

    def project_out(i, b):
        both = jnp.concatenate([mixed[i, 0, rows_of(b)], mixed[i, 1, rows_of(b)]], axis=1)
        x = x_all[i, rows_of(b)].astype(F32)
        return (x + dot(both, w_out[i])).astype(BF16)

    def build(b):
        here = rot_v[b // 4, :, rows_of(b % 4)].astype(F32)
        column = jnp.broadcast_to(here, (BALL, BALL)).T
        for n in range(BALLS):
            ids = (lane + n * BALL).astype(F32)
            perm[rows_of(b), n * BALL : (n + 1) * BALL] = jnp.where(
                ids == column, 1.0, 0.0
            ).astype(BF16)

    def build_t(b):
        ids = lax.broadcasted_iota(jnp.int32, (BALL, ROWS), 0) + b * BALL
        rot_row = jnp.concatenate([rot_v[0], rot_v[1]], axis=1)
        perm_t[rows_of(b)] = jnp.where(ids == rot_row, 1.0, 0.0).astype(BF16)

    kept[0].wait()
    for copy in loads[:3]:
        copy.wait()
    loop(4, lambda j: project(0, c * 4 + j))
    for copy in kept[1:4]:
        copy.wait()
    loop(4, lambda j: build(c * 4 + j))
    pl.semaphore_wait(barrier, near_count + planes - 1)
    for copy in sent:
        copy.start()
    for n in (1, 2, 3):
        sent[n].wait()
    to_smem = pltpu.make_async_copy(lists_v, lists_s, smem_sem)
    to_smem.start()
    sent[0].wait()
    loop(4, lambda j: project(0, other * 4 + j))
    to_smem.wait()
    for copy in loads[3:]:
        copy.wait()

    def attend_send(j):
        attend(0, j)
        mix_copy(0, j, j).start()

    loop(BALLS, attend_send)
    loop(BALLS, build_t)
    loop(4, lambda j: build(other * 4 + j))

    def hidden_rows(b):
        mix_copy(0, b, b).wait()
        x_all[2, rows_of(b)] = project_out(0, b)

    loop(BALLS, hidden_rows)
    x_all[1] = dot(perm[...], x_all[2]).astype(BF16)
    loop(BALLS, lambda b: project(1, b))

    def attend_two(j):
        attend(1, other * 4 + j)
        mix_copy(1, other * 4 + j, j).start()

    loop(4, attend_two)
    loop(4, lambda j: attend(1, c * 4 + j))

    def result_rows(j):
        mix_copy(1, other * 4 + j, j).wait()
        result[0, rows_of(j)] = project_out(1, c * 4 + j)

    kept[4].wait()
    sent[4].wait()

    def attend_back(i, b):
        ids = listed(i, b)
        grads = g_all[i, rows_of(b)]
        own_out = w_out[i, col, :]
        mixed_grad = stacked(dot_nt(grads, own_out)).astype(BF16)
        mixed_grad_t = dot_nt(own_out, grads).astype(BF16).astype(F32)
        product = mixed_grad_t * mix_f[i, :, rows_of(b)]
        half = OWN // 2
        inner = jnp.concatenate(
            [
                jnp.sum(product[:half], axis=0, keepdims=True),
                jnp.sum(product[half:], axis=0, keepdims=True),
            ],
            axis=1,
        )
        values = jnp.concatenate([kv_all[i, t, :, OWN:] for t in ids], axis=0)
        weights = att[i, b]
        scores_grad = jnp.concatenate(
            [
                (
                    weights[:, cols].astype(F32)
                    * (dot_nt(values, mixed_grad[cols]) - inner[:, cols])
                ).astype(BF16)
                for cols in (slice(0, BALL), slice(BALL, 2 * BALL))
            ],
            axis=1,
        )
        values_grad = dot(weights, mixed_grad)
        keys_grad = dot(scores_grad, q_st[i, b])
        for n in range(LISTED):
            parts[b * LISTED + n, :, :OWN] = keys_grad[n * BALL : (n + 1) * BALL]
            parts[b * LISTED + n, :, OWN:] = values_grad[n * BALL : (n + 1) * BALL]
        keys_t = jnp.concatenate([k_t[i, t] for t in ids], axis=1)
        query_grad_t = unstacked_t(dot(keys_t, scores_grad)) * 0.125
        dqkv[rows_of(b), :OWN] = query_grad_t.T.astype(BF16)

    def gather_parts(i, t):
        total = jnp.zeros((BALL, D), F32)
        for b in range(BALLS):
            at = jnp.int32(LISTED * BALLS)
            for n in range(LISTED):
                at = jnp.where(lists_s[i, b // 4, b % 4, n] == t, b * LISTED + n, at)
            total = total + parts[at]
        dqkv[rows_of(t), OWN:] = total.astype(BF16)

    def ng_copy(i, b, slot):
        ref = ngrad.at[i, c, rows_of(b)]
        return remote(ref, ref, ng_send.at[i, slot], ng_recv.at[i, slot])

    def partial_rows(i, b):
        ngrad[i, c, rows_of(b)] = dot_nt(dqkv[rows_of(b)], w_own[i]).astype(BF16)

    def row_grads(i, b):
        x = x_all[i, rows_of(b)].astype(F32)
        gain = gains[i][...].astype(F32).reshape(1, D)
        factor = lax.rsqrt(jnp.mean(x * x, axis=-1, keepdims=True) + EPSILON)
        grad = ngrad[i, 0, rows_of(b)].astype(F32) + ngrad[i, 1, rows_of(b)].astype(F32)
        grad = grad.astype(BF16).astype(F32)
        scaled = grad * gain
        inner = jnp.mean(scaled * x, axis=-1, keepdims=True)
        inputs_grad = factor * scaled - x * (factor * factor * factor) * inner
        rows = (g_all[i, rows_of(b)].astype(F32) + inputs_grad).astype(BF16)
        return rows, jnp.sum(grad * (x * factor), axis=0, keepdims=True)

    class Sum:
        def __init__(self, r, own, arrived, along, full):
            self.r, self.own, self.arrived, self.along, self.full = r, own, arrived, along, full
            at = rows_of(xy, chunk)
            self.first = [
                copy_to(
                    near(k),
                    own.at[rows_of((xy + k) % near_count, chunk)],
                    arrived.at[k - 1],
                    send_xy.at[r, k - 1],
                    recv_xy.at[r, k - 1],
                )
                for k in range(1, near_count)
            ]
            self.second = [
                copy_to(
                    deep(k), along.at[z], along.at[z], send_z.at[r, k - 1], recv_z.at[r, k - 1]
                )
                for k in range(1, planes)
            ]
            mine = full.at[c, at]
            self.third = [
                copy_to(near(k), mine, mine, send_all.at[r, k - 1], recv_all.at[r, k - 1])
                for k in range(1, near_count)
            ]
            pieces = [
                full.at[c, rows_of((xy - k + near_count) % near_count, chunk)]
                for k in range(near_count)
            ]
            self.across = [
                remote(piece, piece, send_core.at[r, k], recv_core.at[r, k])
                for k, piece in enumerate(pieces)
            ]

        def scatter(self):
            for copy in self.first:
                copy.start()

        def plane(self):
            total = self.own[rows_of(xy, chunk)].astype(F32)
            for k, copy in enumerate(self.first):
                copy.wait()
                total = total + self.arrived[k].astype(F32)
            self.along[z] = total.astype(BF16)
            for copy in self.second:
                copy.start()

        def column(self):
            for copy in self.second:
                copy.wait()
            total = self.along[0].astype(F32)
            for k in range(1, planes):
                total = total + self.along[k].astype(F32)
            self.full[c, rows_of(xy, chunk)] = total.astype(BF16)
            for copy in self.third:
                copy.start()
            self.across[0].start()

        def forward(self):
            for k, copy in enumerate(self.third):
                copy.wait_recv()
                self.across[k + 1].start()

        def finish(self):
            for copy in self.third:
                copy.wait_send()
            for copy in self.across:
                copy.wait()

    sum_early = Sum(0, early, near_early, deep_early, full_early)
    sum_late = Sum(1, late, near_late, deep_late, full_late)
    gain_first = [
        copy_to(
            near(k), near_gain.at[xy], near_gain.at[xy], send_xy.at[2, k - 1], recv_xy.at[2, k - 1]
        )
        for k in range(1, near_count)
    ]
    gain_second = [
        copy_to(deep(k), deep_gain.at[z], deep_gain.at[z], send_z.at[2, k - 1], recv_z.at[2, k - 1])
        for k in range(1, planes)
    ]
    gain_across = remote(
        gain_sums.at[c], gain_sums.at[c], send_core.at[2, 0], recv_core.at[2, 0]
    )

    loop(BALLS, lambda b: attend_back(1, b))
    loop(BALLS, lambda t: gather_parts(1, t))

    def partial_two(b):
        partial_rows(1, b)
        ng_copy(1, b, b).start()

    loop(BALLS, partial_two)
    early[:, : 3 * OWN] = dot(normed_t[1], dqkv[...]).astype(BF16)
    out_grad = dot(mix_t[1], g_all[1]).astype(BF16)
    early[:OWN, 3 * OWN : 4 * OWN] = out_grad[:, :OWN]
    early[OWN:, 3 * OWN : 4 * OWN] = out_grad[:, OWN:]

    def rows_two(b, total):
        ng_copy(1, b, b).wait()
        rows, gain_part = row_grads(1, b)
        x_all[2, rows_of(b)] = rows
        mine = ((b // 4) == c).astype(F32)
        return total + gain_part * mine

    gain_two_part = lax.fori_loop(0, BALLS, rows_two, jnp.zeros((1, D), F32), unroll=4)

    g_all[0] = dot(perm_t[...], x_all[2]).astype(BF16)
    out_grad = dot(mix_t[0], g_all[0]).astype(BF16)
    early[:OWN, 4 * OWN :] = out_grad[:, :OWN]
    early[OWN:, 4 * OWN :] = out_grad[:, OWN:]
    sum_early.scatter()
    loop(BALLS, lambda b: attend_back(0, b))
    loop(BALLS, lambda t: gather_parts(0, t))
    late[...] = dot(normed_t[0], dqkv[...]).astype(BF16)
    sum_late.scatter()

    def partial_one(j):
        partial_rows(0, other * 4 + j)
        ng_copy(0, other * 4 + j, j).start()

    loop(4, partial_one)
    loop(4, lambda j: partial_rows(0, c * 4 + j))
    sum_early.plane()

    def rows_one(j, total):
        ng_copy(0, other * 4 + j, j).wait()
        rows, gain_part = row_grads(0, c * 4 + j)
        points_grad[0, rows_of(j)] = rows
        return total + gain_part

    gain_one_part = lax.fori_loop(0, 4, rows_one, jnp.zeros((1, D), F32), unroll=4)
    near_gain[xy] = jnp.concatenate([gain_one_part, gain_two_part], axis=0)
    for copy in gain_first:
        copy.start()
    loop(4, result_rows)
    sum_late.plane()
    for copy in gain_first:
        copy.wait()
    deep_gain[z] = sum(near_gain[k] for k in range(near_count))
    for copy in gain_second:
        copy.start()
    sum_early.column()
    sum_late.column()
    for copy in gain_second:
        copy.wait()
    gain_sums[c] = sum(deep_gain[k] for k in range(planes))
    gain_across.start()
    sum_early.forward()
    sum_late.forward()
    sum_early.finish()
    sum_late.finish()
    gain_across.wait()


def spread_kernel(
    early,
    late,
    gain_sums,
    result_in,
    points_grad_in,
    result,
    points_grad,
    gain_one,
    qkv_one,
    out_one,
    gain_two,
    qkv_two,
    out_two,
):
    result[...] = result_in[...]
    points_grad[...] = points_grad_in[...]
    for core in range(2):
        here = slice(core * OWN, (core + 1) * OWN)
        for n in range(3):
            into = slice(n * D + core * OWN, n * D + (core + 1) * OWN)
            qkv_one[:, into] = late[core, :, n * OWN : (n + 1) * OWN].astype(F32)
            qkv_two[:, into] = early[core, :, n * OWN : (n + 1) * OWN].astype(F32)
        for at, out in ((4 * OWN, out_one), (3 * OWN, out_two)):
            out[here, :OWN] = early[core, :OWN, at : at + OWN].astype(F32)
            out[here, OWN:] = early[core, OWN:, at : at + OWN].astype(F32)
    gains = gain_sums[0] + gain_sums[1]
    gain_one[...] = gains[0]
    gain_two[...] = gains[1]


def vmem():
    return pl.BlockSpec(memory_space=pltpu.VMEM)


def hbm():
    return pl.BlockSpec(memory_space=pltpu.HBM)


def layers_call(near_count, planes, *args):
    chunk = D // near_count
    peers = max(near_count - 1, 1)
    deeper = max(planes - 1, 1)
    return pl.pallas_call(
        functools.partial(layers_kernel, near_count, planes),
        name="layers",
        out_shape=(
            jax.ShapeDtypeStruct((1, HALF, D), BF16),
            jax.ShapeDtypeStruct((1, HALF, D), BF16),
            jax.ShapeDtypeStruct((2, D, 5 * OWN), BF16),
            jax.ShapeDtypeStruct((2, D, 3 * OWN), BF16),
            jax.ShapeDtypeStruct((2, 2, D), F32),
        ),
        in_specs=[hbm()] * 5 + [vmem(), hbm(), hbm()] * 2,
        out_specs=(vmem(),) * 5,
        scratch_shapes=[
            pltpu.VMEM((3, ROWS, D), BF16),
            pltpu.VMEM((2, ROWS, D), BF16),
            pltpu.VMEM((2, 2, 4, LISTED), jnp.int32),
            pltpu.SMEM((2, 2, 4, LISTED), jnp.int32),
            pltpu.VMEM((2, 1, HALF), jnp.int32),
            pltpu.VMEM((2, D, 3 * OWN), BF16),
            pltpu.VMEM((2, D, D), BF16),
            pltpu.VMEM((2, D, ROWS), BF16),
            pltpu.VMEM((2, BALLS, 2 * BALL, OWN), BF16),
            pltpu.VMEM((2, BALLS, BALL, 2 * OWN), BF16),
            pltpu.VMEM((2, BALLS, OWN, BALL), BF16),
            pltpu.VMEM((2, BALLS, OWN, BALL), BF16),
            pltpu.VMEM((2, BALLS, LISTED * BALL, 2 * BALL), BF16),
            pltpu.VMEM((2, OWN, ROWS), BF16),
            pltpu.VMEM((2, OWN, ROWS), F32),
            pltpu.VMEM((2, 2, ROWS, OWN), BF16),
            pltpu.VMEM((ROWS, 3 * OWN), BF16),
            pltpu.VMEM((LISTED * BALLS + 1, BALL, D), F32),
            pltpu.VMEM((2, 2, ROWS, D), BF16),
            pltpu.VMEM((ROWS, ROWS), BF16),
            pltpu.VMEM((ROWS, ROWS), BF16),
            pltpu.VMEM((D, 5 * OWN), BF16),
            pltpu.VMEM((D, 3 * OWN), BF16),
            pltpu.VMEM((peers, chunk, 5 * OWN), BF16),
            pltpu.VMEM((peers, chunk, 3 * OWN), BF16),
            pltpu.VMEM((planes, chunk, 5 * OWN), BF16),
            pltpu.VMEM((planes, chunk, 3 * OWN), BF16),
            pltpu.VMEM((near_count, 2, D), F32),
            pltpu.VMEM((planes, 2, D), F32),
            pltpu.SemaphoreType.DMA((5,)),
            pltpu.SemaphoreType.DMA((5,)),
            pltpu.SemaphoreType.DMA((5,)),
            pltpu.SemaphoreType.DMA((8,)),
            pltpu.SemaphoreType.DMA,
            pltpu.SemaphoreType.DMA((2, BALLS)),
            pltpu.SemaphoreType.DMA((2, BALLS)),
            pltpu.SemaphoreType.DMA((2, BALLS)),
            pltpu.SemaphoreType.DMA((2, BALLS)),
            pltpu.SemaphoreType.DMA((3, peers)),
            pltpu.SemaphoreType.DMA((3, peers)),
            pltpu.SemaphoreType.DMA((3, deeper)),
            pltpu.SemaphoreType.DMA((3, deeper)),
            pltpu.SemaphoreType.DMA((2, peers)),
            pltpu.SemaphoreType.DMA((2, peers)),
            pltpu.SemaphoreType.DMA((3, near_count)),
            pltpu.SemaphoreType.DMA((3, near_count)),
        ],
        compiler_params=pltpu.CompilerParams(
            collective_id=0, has_side_effects=True, vmem_limit_bytes=56 << 20
        ),
    )(*args)


def spread_call(early, late, gain_sums, result, points_grad):
    shapes = (
        jax.ShapeDtypeStruct((D,), F32),
        jax.ShapeDtypeStruct((D, 3 * D), F32),
        jax.ShapeDtypeStruct((D, D), F32),
    )
    rows = jax.ShapeDtypeStruct((1, HALF, D), BF16)
    return pl.pallas_call(
        spread_kernel,
        name="spread",
        out_shape=(rows, rows) + shapes + shapes,
        in_specs=[vmem()] * 5,
        out_specs=(vmem(),) * 8,
        compiler_params=pltpu.CompilerParams(vmem_limit_bytes=16 << 20),
    )(early, late, gain_sums, result, points_grad)


def local(*args):
    planes = lax.axis_size("geo") // XY
    result, points_grad, early, late, gain_sums = layers_call(XY, planes, *args)
    return spread_call(early, late, gain_sums, result, points_grad)


def solution(mesh):
    rows = P("geo", "pts", None)
    placed = (rows, rows, rows, rows, P("geo", "pts"), P(), P(), P(), P(), P(), P())
    return jax.shard_map(
        local,
        mesh=mesh,
        in_specs=placed,
        out_specs=(rows, rows, P(), P(), P(), P(), P(), P()),
        check_vma=False,
    )
```

```python
import functools

import jax
import jax.numpy as jnp
from jax import lax
from jax.experimental import pallas as pl
from jax.experimental.pallas import tpu as pltpu
from jax.sharding import PartitionSpec as P

HEADS = 4
BALL = 128
LISTED = 4
BALLS = 8
ROWS = BALL * BALLS
HALF = ROWS // 2
D = 256
OWN = 128
EPSILON = 1e-06
XY = 16
MESH = pl.DeviceIdType.MESH
F32 = jnp.float32
BF16 = jnp.bfloat16


def dot(a, b):
    return jnp.dot(a, b, preferred_element_type=F32)


def dot_nt(a, b):
    return lax.dot_general(a, b, (((1,), (1,)), ((), ())), preferred_element_type=F32)


def rows_of(b, size=BALL):
    return pl.ds(pl.multiple_of(b * size, size), size)


def layers_kernel(
    near_count,
    planes,
    points,
    result_grad,
    lists_one,
    lists_two,
    rotation,
    gain_one,
    qkv_one,
    out_one,
    gain_two,
    qkv_two,
    out_two,
    result,
    points_grad,
    full_early,
    full_late,
    gain_sums,
    x_all,
    g_all,
    lists_v,
    lists_s,
    rot_v,
    w_own,
    w_out,
    normed_t,
    q_st,
    kv_all,
    k_t,
    v_t,
    att,
    mix_t,
    mix_f,
    mixed,
    dqkv,
    parts,
    ngrad,
    perm,
    perm_t,
    early,
    late,
    near_early,
    near_late,
    deep_early,
    deep_late,
    near_gain,
    deep_gain,
    in_send,
    in_recv,
    own_sem,
    load_sem,
    smem_sem,
    mix_send,
    mix_recv,
    ng_send,
    ng_recv,
    send_xy,
    recv_xy,
    send_z,
    recv_z,
    send_all,
    recv_all,
    send_core,
    recv_core,
):
    c = lax.axis_index("pts")
    other = 1 - c
    geo = lax.axis_index("geo")
    z = geo // near_count
    xy = geo % near_count
    chunk = D // near_count
    gains = (gain_one, gain_two)
    qkvs = (qkv_one, qkv_two)
    outs = (out_one, out_two)

    def copy_to(device, src, dst, send, recv):
        return pltpu.make_async_remote_copy(
            src_ref=src,
            dst_ref=dst,
            send_sem=send,
            recv_sem=recv,
            device_id=device,
            device_id_type=MESH,
        )

    def remote(src, dst, send, recv):
        return copy_to({"pts": other}, src, dst, send, recv)

    def near(k):
        return {"geo": z * near_count + (xy + k) % near_count}

    def deep(k):
        return {"geo": ((z + k) % planes) * near_count + xy}

    barrier = pltpu.get_barrier_semaphore()
    pl.semaphore_signal(barrier, inc=1, device_id={"pts": other}, device_id_type=MESH)
    for k in range(1, near_count):
        pl.semaphore_signal(barrier, inc=1, device_id=near(k), device_id_type=MESH)
    for k in range(1, planes):
        pl.semaphore_signal(barrier, inc=1, device_id=deep(k), device_id_type=MESH)

    inputs = (
        (points.at[0], x_all.at[0, rows_of(c, HALF)]),
        (lists_one.at[0], lists_v.at[0, c]),
        (lists_two.at[0], lists_v.at[1, c]),
        (rotation, rot_v.at[c]),
        (result_grad.at[0], g_all.at[1, rows_of(c, HALF)]),
    )
    kept = [
        pltpu.make_async_copy(src, dst, own_sem.at[n]) for n, (src, dst) in enumerate(inputs)
    ]
    sent = [
        remote(src, dst, in_send.at[n], in_recv.at[n]) for n, (src, dst) in enumerate(inputs)
    ]
    loads = []
    for i in range(2):
        for n in range(3):
            part = pl.ds(pl.multiple_of(n * D + c * OWN, OWN), OWN)
            loads.append(
                pltpu.make_async_copy(
                    qkvs[i].at[:, part],
                    w_own.at[i, :, n * OWN : (n + 1) * OWN],
                    load_sem.at[4 * i + n],
                )
            )
        loads.append(pltpu.make_async_copy(outs[i], w_out.at[i], load_sem.at[4 * i + 3]))
    kept[0].start()
    for copy in loads[:3]:
        copy.start()
    for copy in kept[1:] + loads[3:]:
        copy.start()
    parts[LISTED * BALLS] = jnp.zeros((BALL, D), F32)
    col = pl.ds(pl.multiple_of(c * OWN, OWN), OWN)

    lane = lax.broadcasted_iota(jnp.int32, (BALL, OWN), 1)
    first = lane < OWN // 2

    def stacked(value):
        zero = jnp.zeros_like(value)
        return jnp.concatenate(
            [jnp.where(first, value, zero), jnp.where(first, zero, value)], axis=0
        )

    def unstacked_t(value):
        return jnp.concatenate([value[: OWN // 2, :BALL], value[OWN // 2 :, BALL:]], axis=0)

    def project(i, b):
        x = x_all[i, rows_of(b)].astype(F32)
        gain = gains[i][...].astype(F32).reshape(1, D)
        factor = lax.rsqrt(jnp.mean(x * x, axis=-1, keepdims=True) + EPSILON)
        normed = x * factor * gain
        normed_t[i, :, rows_of(b)] = normed.T.astype(BF16)
        qkv = dot(normed.astype(BF16), w_own[i])
        q = qkv[:, :OWN].astype(BF16).astype(F32) * 0.125
        q_st[i, b] = stacked(q).astype(BF16)
        kv_all[i, b] = qkv[:, OWN:].astype(BF16)
        k_t[i, b] = qkv[:, OWN : 2 * OWN].T.astype(BF16)
        v_t[i, b] = qkv[:, 2 * OWN :].T.astype(BF16)

    def listed(i, b):
        return [lists_s[i, b // 4, b % 4, n] for n in range(LISTED)]

    def attend(i, b):
        ids = listed(i, b)
        queries = q_st[i, b]
        scores = [dot_nt(kv_all[i, t, :, :OWN], queries) for t in ids]
        top = jnp.maximum(jnp.maximum(scores[0], scores[1]), jnp.maximum(scores[2], scores[3]))
        top = jnp.max(top, axis=0, keepdims=True)
        exponents = [jnp.exp(score - top) for score in scores]
        total = (exponents[0] + exponents[1]) + (exponents[2] + exponents[3])
        scale = 1.0 / jnp.sum(total, axis=0, keepdims=True)
        weights = [(exponent * scale).astype(BF16) for exponent in exponents]
        for n in range(LISTED):
            att[i, b, n * BALL : (n + 1) * BALL] = weights[n]
        values_t = jnp.concatenate([v_t[i, t] for t in ids], axis=1)
        own_t = unstacked_t(dot(values_t, jnp.concatenate(weights, axis=0)))
        mix_f[i, :, rows_of(b)] = own_t
        mix_t[i, :, rows_of(b)] = own_t.astype(BF16)
        mixed[i, c, rows_of(b)] = own_t.T.astype(BF16)

    def loop(count, body, unroll=4):
        lax.fori_loop(0, count, lambda j, _: body(j), None, unroll=unroll)

    def mix_copy(i, b, slot):
        ref = mixed.at[i, c, rows_of(b)]
        return remote(ref, ref, mix_send.at[i, slot], mix_recv.at[i, slot])

    def project_out(i, b):
        both = jnp.concatenate([mixed[i, 0, rows_of(b)], mixed[i, 1, rows_of(b)]], axis=1)
        x = x_all[i, rows_of(b)].astype(F32)
        return (x + dot(both, w_out[i])).astype(BF16)

    def build(b):
        here = rot_v[b // 4, :, rows_of(b % 4)].astype(F32)
        column = jnp.broadcast_to(here, (BALL, BALL)).T
        for n in range(BALLS):
            ids = (lane + n * BALL).astype(F32)
            perm[rows_of(b), n * BALL : (n + 1) * BALL] = jnp.where(
                ids == column, 1.0, 0.0
            ).astype(BF16)

    def build_t(b):
        ids = lax.broadcasted_iota(jnp.int32, (BALL, ROWS), 0) + b * BALL
        rot_row = jnp.concatenate([rot_v[0], rot_v[1]], axis=1)
        perm_t[rows_of(b)] = jnp.where(ids == rot_row, 1.0, 0.0).astype(BF16)

    kept[0].wait()
    for copy in loads[:3]:
        copy.wait()
    loop(4, lambda j: project(0, c * 4 + j))
    for copy in kept[1:4]:
        copy.wait()
    loop(4, lambda j: build(c * 4 + j))
    pl.semaphore_wait(barrier, near_count + planes - 1)
    for copy in sent:
        copy.start()
    for n in (1, 2, 3):
        sent[n].wait()
    to_smem = pltpu.make_async_copy(lists_v, lists_s, smem_sem)
    to_smem.start()
    sent[0].wait()
    loop(4, lambda j: project(0, other * 4 + j))
    to_smem.wait()
    for copy in loads[3:]:
        copy.wait()

    def attend_send(j):
        attend(0, j)
        mix_copy(0, j, j).start()

    loop(BALLS, attend_send)
    loop(BALLS, build_t)
    loop(4, lambda j: build(other * 4 + j))

    def hidden_rows(b):
        mix_copy(0, b, b).wait()
        x_all[2, rows_of(b)] = project_out(0, b)

    loop(BALLS, hidden_rows)
    x_all[1] = dot(perm[...], x_all[2]).astype(BF16)
    loop(BALLS, lambda b: project(1, b))

    def attend_two(j):
        attend(1, other * 4 + j)
        mix_copy(1, other * 4 + j, j).start()

    loop(4, attend_two)
    loop(4, lambda j: attend(1, c * 4 + j))

    def result_rows(j):
        mix_copy(1, other * 4 + j, j).wait()
        result[0, rows_of(j)] = project_out(1, c * 4 + j)

    kept[4].wait()
    sent[4].wait()

    def attend_back(i, b):
        ids = listed(i, b)
        grads = g_all[i, rows_of(b)]
        own_out = w_out[i, col, :]
        mixed_grad = stacked(dot_nt(grads, own_out)).astype(BF16)
        mixed_grad_t = dot_nt(own_out, grads).astype(BF16).astype(F32)
        product = mixed_grad_t * mix_f[i, :, rows_of(b)]
        half = OWN // 2
        inner = jnp.concatenate(
            [
                jnp.sum(product[:half], axis=0, keepdims=True),
                jnp.sum(product[half:], axis=0, keepdims=True),
            ],
            axis=1,
        )
        values = jnp.concatenate([kv_all[i, t, :, OWN:] for t in ids], axis=0)
        weights = att[i, b]
        scores_grad = jnp.concatenate(
            [
                (
                    weights[:, cols].astype(F32)
                    * (dot_nt(values, mixed_grad[cols]) - inner[:, cols])
                ).astype(BF16)
                for cols in (slice(0, BALL), slice(BALL, 2 * BALL))
            ],
            axis=1,
        )
        values_grad = dot(weights, mixed_grad)
        keys_grad = dot(scores_grad, q_st[i, b])
        for n in range(LISTED):
            parts[b * LISTED + n, :, :OWN] = keys_grad[n * BALL : (n + 1) * BALL]
            parts[b * LISTED + n, :, OWN:] = values_grad[n * BALL : (n + 1) * BALL]
        keys_t = jnp.concatenate([k_t[i, t] for t in ids], axis=1)
        query_grad_t = unstacked_t(dot(keys_t, scores_grad)) * 0.125
        dqkv[rows_of(b), :OWN] = query_grad_t.T.astype(BF16)

    def gather_parts(i, t):
        total = jnp.zeros((BALL, D), F32)
        for b in range(BALLS):
            at = jnp.int32(LISTED * BALLS)
            for n in range(LISTED):
                at = jnp.where(lists_s[i, b // 4, b % 4, n] == t, b * LISTED + n, at)
            total = total + parts[at]
        dqkv[rows_of(t), OWN:] = total.astype(BF16)

    def ng_copy(i, b, slot):
        ref = ngrad.at[i, c, rows_of(b)]
        return remote(ref, ref, ng_send.at[i, slot], ng_recv.at[i, slot])

    def partial_rows(i, b):
        ngrad[i, c, rows_of(b)] = dot_nt(dqkv[rows_of(b)], w_own[i]).astype(BF16)

    def row_grads(i, b):
        x = x_all[i, rows_of(b)].astype(F32)
        gain = gains[i][...].astype(F32).reshape(1, D)
        factor = lax.rsqrt(jnp.mean(x * x, axis=-1, keepdims=True) + EPSILON)
        grad = ngrad[i, 0, rows_of(b)].astype(F32) + ngrad[i, 1, rows_of(b)].astype(F32)
        grad = grad.astype(BF16).astype(F32)
        scaled = grad * gain
        inner = jnp.mean(scaled * x, axis=-1, keepdims=True)
        inputs_grad = factor * scaled - x * (factor * factor * factor) * inner
        rows = (g_all[i, rows_of(b)].astype(F32) + inputs_grad).astype(BF16)
        return rows, jnp.sum(grad * (x * factor), axis=0, keepdims=True)

    class Sum:
        def __init__(self, r, own, arrived, along, full):
            self.r, self.own, self.arrived, self.along, self.full = r, own, arrived, along, full
            at = rows_of(xy, chunk)
            self.first = [
                copy_to(
                    near(k),
                    own.at[rows_of((xy + k) % near_count, chunk)],
                    arrived.at[k - 1],
                    send_xy.at[r, k - 1],
                    recv_xy.at[r, k - 1],
                )
                for k in range(1, near_count)
            ]
            self.second = [
                copy_to(
                    deep(k), along.at[z], along.at[z], send_z.at[r, k - 1], recv_z.at[r, k - 1]
                )
                for k in range(1, planes)
            ]
            mine = full.at[c, at]
            self.third = [
                copy_to(near(k), mine, mine, send_all.at[r, k - 1], recv_all.at[r, k - 1])
                for k in range(1, near_count)
            ]
            pieces = [
                full.at[c, rows_of((xy - k + near_count) % near_count, chunk)]
                for k in range(near_count)
            ]
            self.across = [
                remote(piece, piece, send_core.at[r, k], recv_core.at[r, k])
                for k, piece in enumerate(pieces)
            ]

        def scatter(self):
            for copy in self.first:
                copy.start()

        def plane(self):
            total = self.own[rows_of(xy, chunk)].astype(F32)
            for k, copy in enumerate(self.first):
                copy.wait()
                total = total + self.arrived[k].astype(F32)
            self.along[z] = total.astype(BF16)
            for copy in self.second:
                copy.start()

        def column(self):
            for copy in self.second:
                copy.wait()
            total = self.along[0].astype(F32)
            for k in range(1, planes):
                total = total + self.along[k].astype(F32)
            self.full[c, rows_of(xy, chunk)] = total.astype(BF16)
            for copy in self.third:
                copy.start()
            self.across[0].start()

        def forward(self):
            for k, copy in enumerate(self.third):
                copy.wait_recv()
                self.across[k + 1].start()

        def finish(self):
            for copy in self.third:
                copy.wait_send()
            for copy in self.across:
                copy.wait()

    sum_early = Sum(0, early, near_early, deep_early, full_early)
    sum_late = Sum(1, late, near_late, deep_late, full_late)
    gain_first = [
        copy_to(
            near(k), near_gain.at[xy], near_gain.at[xy], send_xy.at[2, k - 1], recv_xy.at[2, k - 1]
        )
        for k in range(1, near_count)
    ]
    gain_second = [
        copy_to(deep(k), deep_gain.at[z], deep_gain.at[z], send_z.at[2, k - 1], recv_z.at[2, k - 1])
        for k in range(1, planes)
    ]
    gain_across = remote(
        gain_sums.at[c], gain_sums.at[c], send_core.at[2, 0], recv_core.at[2, 0]
    )

    loop(BALLS, lambda b: attend_back(1, b))
    loop(BALLS, lambda t: gather_parts(1, t))

    def partial_two(b):
        partial_rows(1, b)
        ng_copy(1, b, b).start()

    loop(BALLS, partial_two)
    early[:, : 3 * OWN] = dot(normed_t[1], dqkv[...]).astype(BF16)
    out_grad = dot(mix_t[1], g_all[1]).astype(BF16)
    early[:OWN, 3 * OWN : 4 * OWN] = out_grad[:, :OWN]
    early[OWN:, 3 * OWN : 4 * OWN] = out_grad[:, OWN:]

    def rows_two(b, total):
        ng_copy(1, b, b).wait()
        rows, gain_part = row_grads(1, b)
        x_all[2, rows_of(b)] = rows
        mine = ((b // 4) == c).astype(F32)
        return total + gain_part * mine

    gain_two_part = lax.fori_loop(0, BALLS, rows_two, jnp.zeros((1, D), F32), unroll=4)

    g_all[0] = dot(perm_t[...], x_all[2]).astype(BF16)
    out_grad = dot(mix_t[0], g_all[0]).astype(BF16)
    early[:OWN, 4 * OWN :] = out_grad[:, :OWN]
    early[OWN:, 4 * OWN :] = out_grad[:, OWN:]
    sum_early.scatter()
    loop(BALLS, lambda b: attend_back(0, b))
    loop(BALLS, lambda t: gather_parts(0, t))
    late[...] = dot(normed_t[0], dqkv[...]).astype(BF16)
    sum_late.scatter()
    sum_early.plane()

    def partial_one(j):
        partial_rows(0, other * 4 + j)
        ng_copy(0, other * 4 + j, j).start()

    loop(4, partial_one)
    loop(4, lambda j: partial_rows(0, c * 4 + j))

    def rows_one(j, total):
        ng_copy(0, other * 4 + j, j).wait()
        rows, gain_part = row_grads(0, c * 4 + j)
        points_grad[0, rows_of(j)] = rows
        return total + gain_part

    gain_one_part = lax.fori_loop(0, 4, rows_one, jnp.zeros((1, D), F32), unroll=4)
    near_gain[xy] = jnp.concatenate([gain_one_part, gain_two_part], axis=0)
    for copy in gain_first:
        copy.start()
    loop(4, result_rows)
    sum_late.plane()
    for copy in gain_first:
        copy.wait()
    deep_gain[z] = sum(near_gain[k] for k in range(near_count))
    for copy in gain_second:
        copy.start()
    sum_early.column()
    sum_late.column()
    for copy in gain_second:
        copy.wait()
    gain_sums[c] = sum(deep_gain[k] for k in range(planes))
    gain_across.start()
    sum_early.forward()
    sum_late.forward()
    sum_early.finish()
    sum_late.finish()
    gain_across.wait()


def spread_kernel(
    early,
    late,
    gain_sums,
    result_in,
    points_grad_in,
    result,
    points_grad,
    gain_one,
    qkv_one,
    out_one,
    gain_two,
    qkv_two,
    out_two,
):
    result[...] = result_in[...]
    points_grad[...] = points_grad_in[...]
    for core in range(2):
        here = slice(core * OWN, (core + 1) * OWN)
        for n in range(3):
            into = slice(n * D + core * OWN, n * D + (core + 1) * OWN)
            qkv_one[:, into] = late[core, :, n * OWN : (n + 1) * OWN].astype(F32)
            qkv_two[:, into] = early[core, :, n * OWN : (n + 1) * OWN].astype(F32)
        for at, out in ((4 * OWN, out_one), (3 * OWN, out_two)):
            out[here, :OWN] = early[core, :OWN, at : at + OWN].astype(F32)
            out[here, OWN:] = early[core, OWN:, at : at + OWN].astype(F32)
    gains = gain_sums[0] + gain_sums[1]
    gain_one[...] = gains[0]
    gain_two[...] = gains[1]


def vmem():
    return pl.BlockSpec(memory_space=pltpu.VMEM)


def hbm():
    return pl.BlockSpec(memory_space=pltpu.HBM)


def layers_call(near_count, planes, *args):
    chunk = D // near_count
    peers = max(near_count - 1, 1)
    deeper = max(planes - 1, 1)
    return pl.pallas_call(
        functools.partial(layers_kernel, near_count, planes),
        name="layers",
        out_shape=(
            jax.ShapeDtypeStruct((1, HALF, D), BF16),
            jax.ShapeDtypeStruct((1, HALF, D), BF16),
            jax.ShapeDtypeStruct((2, D, 5 * OWN), BF16),
            jax.ShapeDtypeStruct((2, D, 3 * OWN), BF16),
            jax.ShapeDtypeStruct((2, 2, D), F32),
        ),
        in_specs=[hbm()] * 5 + [vmem(), hbm(), hbm()] * 2,
        out_specs=(vmem(),) * 5,
        scratch_shapes=[
            pltpu.VMEM((3, ROWS, D), BF16),
            pltpu.VMEM((2, ROWS, D), BF16),
            pltpu.VMEM((2, 2, 4, LISTED), jnp.int32),
            pltpu.SMEM((2, 2, 4, LISTED), jnp.int32),
            pltpu.VMEM((2, 1, HALF), jnp.int32),
            pltpu.VMEM((2, D, 3 * OWN), BF16),
            pltpu.VMEM((2, D, D), BF16),
            pltpu.VMEM((2, D, ROWS), BF16),
            pltpu.VMEM((2, BALLS, 2 * BALL, OWN), BF16),
            pltpu.VMEM((2, BALLS, BALL, 2 * OWN), BF16),
            pltpu.VMEM((2, BALLS, OWN, BALL), BF16),
            pltpu.VMEM((2, BALLS, OWN, BALL), BF16),
            pltpu.VMEM((2, BALLS, LISTED * BALL, 2 * BALL), BF16),
            pltpu.VMEM((2, OWN, ROWS), BF16),
            pltpu.VMEM((2, OWN, ROWS), F32),
            pltpu.VMEM((2, 2, ROWS, OWN), BF16),
            pltpu.VMEM((ROWS, 3 * OWN), BF16),
            pltpu.VMEM((LISTED * BALLS + 1, BALL, D), F32),
            pltpu.VMEM((2, 2, ROWS, D), BF16),
            pltpu.VMEM((ROWS, ROWS), BF16),
            pltpu.VMEM((ROWS, ROWS), BF16),
            pltpu.VMEM((D, 5 * OWN), BF16),
            pltpu.VMEM((D, 3 * OWN), BF16),
            pltpu.VMEM((peers, chunk, 5 * OWN), BF16),
            pltpu.VMEM((peers, chunk, 3 * OWN), BF16),
            pltpu.VMEM((planes, chunk, 5 * OWN), BF16),
            pltpu.VMEM((planes, chunk, 3 * OWN), BF16),
            pltpu.VMEM((near_count, 2, D), F32),
            pltpu.VMEM((planes, 2, D), F32),
            pltpu.SemaphoreType.DMA((5,)),
            pltpu.SemaphoreType.DMA((5,)),
            pltpu.SemaphoreType.DMA((5,)),
            pltpu.SemaphoreType.DMA((8,)),
            pltpu.SemaphoreType.DMA,
            pltpu.SemaphoreType.DMA((2, BALLS)),
            pltpu.SemaphoreType.DMA((2, BALLS)),
            pltpu.SemaphoreType.DMA((2, BALLS)),
            pltpu.SemaphoreType.DMA((2, BALLS)),
            pltpu.SemaphoreType.DMA((3, peers)),
            pltpu.SemaphoreType.DMA((3, peers)),
            pltpu.SemaphoreType.DMA((3, deeper)),
            pltpu.SemaphoreType.DMA((3, deeper)),
            pltpu.SemaphoreType.DMA((2, peers)),
            pltpu.SemaphoreType.DMA((2, peers)),
            pltpu.SemaphoreType.DMA((3, near_count)),
            pltpu.SemaphoreType.DMA((3, near_count)),
        ],
        compiler_params=pltpu.CompilerParams(
            collective_id=0, has_side_effects=True, vmem_limit_bytes=56 << 20
        ),
    )(*args)


def spread_call(early, late, gain_sums, result, points_grad):
    shapes = (
        jax.ShapeDtypeStruct((D,), F32),
        jax.ShapeDtypeStruct((D, 3 * D), F32),
        jax.ShapeDtypeStruct((D, D), F32),
    )
    rows = jax.ShapeDtypeStruct((1, HALF, D), BF16)
    return pl.pallas_call(
        spread_kernel,
        name="spread",
        out_shape=(rows, rows) + shapes + shapes,
        in_specs=[vmem()] * 5,
        out_specs=(vmem(),) * 8,
        compiler_params=pltpu.CompilerParams(vmem_limit_bytes=16 << 20),
    )(early, late, gain_sums, result, points_grad)


def local(*args):
    planes = lax.axis_size("geo") // XY
    result, points_grad, early, late, gain_sums = layers_call(XY, planes, *args)
    return spread_call(early, late, gain_sums, result, points_grad)


def solution(mesh):
    rows = P("geo", "pts", None)
    placed = (rows, rows, rows, rows, P("geo", "pts"), P(), P(), P(), P(), P(), P())
    return jax.shard_map(
        local,
        mesh=mesh,
        in_specs=placed,
        out_specs=(rows, rows, P(), P(), P(), P(), P(), P()),
        check_vma=False,
    )
```
